32 devices in a mesh: dp: 4 (over x, core), ctx: 8 (over z, y).
Axes of the slice: x: 2, y: 2, z: 4, core: 2. Of those that a mesh axis runs over, the one named last changes fastest.
Arguments:
- inputs: bfloat16 [12, 1024, 960], P('dp', 'ctx'), may hold values from -6 to 6
- gain_one: bfloat16 [960], P('ctx'), may hold values from 0.099609375 to 1.8984375
- query_weight: bfloat16 [960, 960], P('dp', 'ctx'), may hold values from -0.1875 to 0.1875
- key_weight: bfloat16 [960, 320], P('dp', 'ctx'), may hold values from -0.1875 to 0.1875
- value_weight: bfloat16 [960, 320], P('dp', 'ctx'), may hold values from -0.1875 to 0.1875
- output_weight: bfloat16 [960, 960], P('dp', 'ctx'), may hold values from -1.5 to 1.5
- gain_two: bfloat16 [960], P('ctx'), may hold values from 0.099609375 to 1.8984375
- gate_weight: bfloat16 [960, 2560], P('dp', 'ctx'), may hold values from -0.1875 to 0.1875
- up_weight: bfloat16 [960, 2560], P('dp', 'ctx'), may hold values from -0.1875 to 0.1875
- down_weight: bfloat16 [2560, 960], P('dp', 'ctx'), may hold values from -0.25 to 0.25
- segment_ids: int32 [12, 1024], P('dp', 'ctx'), may hold values from 0 to 3, never falling along the last dimension, each value on 1 to 512 neighbouring positions
- cotangent: bfloat16 [12, 1024, 960], P('dp', 'ctx'), may hold values from -6 to 6
Outputs:
- output: bfloat16 [12, 1024, 960], P('dp', 'ctx')
- input_grad: bfloat16 [12, 1024, 960], P('dp', 'ctx')
- gain_one_grad: float32 [960], P('ctx')
- w_query_grad: float32 [960, 960], P('dp', 'ctx')
- w_key_grad: float32 [960, 320], P('dp', 'ctx')
- w_value_grad: float32 [960, 320], P('dp', 'ctx')
- w_out_grad: float32 [960, 960], P('dp', 'ctx')
- gain_two_grad: float32 [960], P('ctx')
- w_gate_grad: float32 [960, 2560], P('dp', 'ctx')
- w_up_grad: float32 [960, 2560], P('dp', 'ctx')
- w_down_grad: float32 [2560, 960], P('dp', 'ctx')
The draws below stay inside these ranges and needn't reach their ends.
Inputs may be any that keep to these rules, and one draw needn't show every extreme that they name: `segment_ids`: along each sequence the ids never fall; each id marks one document of 1 to 512 tokens, and some document has exactly 512.
All inputs are finite; a program needn't handle non-finite values.
Results may differ from the reference program's by a relative error of at most 0.023.
Values may be sent and summed in bfloat16 or wider, within the bound.
No kernel may reach another device: no remote copies, remote signals or barrier semaphores. Data moves between devices by JAX's collectives and lax.ppermute only.
A program may use at most 192 MiB of HBM per device.

```python
import math
import jax
import jax.numpy as jnp
import numpy as np
from jax import lax

MODEL_DIM = 960
QUERY_HEADS = 15
KEY_VALUE_HEADS = 5
HEAD_DIM = 64
FF = 2560
LENGTH = 1024
SEQS = 12
DOC_MAX = 512
DOCS = 4


def raised(entries, stream_key, source, target, shards_of, factor):
    def block_of(dim):
        return (jnp.arange(entries.shape[dim]) // (entries.shape[dim] // shards_of)).reshape((-1,) + (1,) * (entries.ndim - 1 - dim))

    first = jax.random.permutation(stream_key, shards_of)[block_of(target)]
    far = (block_of(target) + shards_of // 2) % shards_of
    return jnp.where((block_of(source) == first) | (block_of(source) == far), factor * entries, entries)


def block_levels(stream_key, shape, cuts, least, largest):
    def one(dim, shards_of):
        steps = jax.random.uniform(jax.random.fold_in(jax.random.fold_in(stream_key, 6), dim), (shards_of,), jnp.float32, least / len(cuts), largest / len(cuts))
        return jnp.repeat(jnp.exp(steps), shape[dim] // shards_of).reshape((-1,) + (1,) * (len(shape) - dim - 1))

    factor_of = one(*cuts[0])
    for cut in cuts[1:]:
        factor_of = factor_of * one(*cut)
    return factor_of


def profile(count, total, bound, lean):
    portions = [(1 << 20) // math.isqrt(grade ** lean) + 1 for grade in range(2, count + 1)]
    surplus, holding = total - bound - (count - 1), [1] * (count - 1)
    while surplus > 0:
        movable = [i for i in range(count - 1) if holding[i] < bound]
        mass, remaining = sum([portions[i] for i in movable]), surplus
        for i in movable:
            more = min(bound - holding[i], max(1, remaining * portions[i] // mass), surplus)
            holding[i] = holding[i] + more
            surplus = surplus - more
    return np.array([bound] + holding)


def ragged_sizes(key, number_of, total, bound, slope):
    if number_of == 2:
        one = jax.random.randint(key, (), max(1, total - bound), min(bound, total - 1) + 1)
        return jnp.stack([one, total - one])
    sizes = jnp.asarray(profile(number_of, total, bound, slope), jnp.int32)
    twos = (number_of - 1) // 2
    donor, sink = sizes[1:1 + 2 * twos:2], sizes[2:2 + 2 * twos:2]
    margin = jnp.minimum(donor - 1, bound - sink)
    passed = jax.random.randint(jax.random.fold_in(key, 1), (twos,), 0, 1 << 20) % (margin + 1)
    sizes = sizes.at[1:1 + 2 * twos:2].set(donor - passed).at[2:2 + 2 * twos:2].set(sink + passed)
    return sizes[jax.random.permutation(jax.random.fold_in(key, 2), number_of)]


def scatter_about(own_key, dims, scale, bound, cuts=(), kind=jnp.bfloat16):
    values = scale * jax.random.normal(own_key, dims, jnp.float32)
    if cuts:
        values = values * block_levels(own_key, dims, cuts, -0.22, 0.18)
    return jnp.clip(values, -bound, bound).astype(kind)


def gaussian_with(stream_key, shape, spread, bound, split, heavy, kind=jnp.bfloat16):
    array = spread * jax.random.normal(stream_key, shape, jnp.float32)
    if split:
        array = array * block_levels(stream_key, shape, split, -0.22, 0.18)
    return jnp.clip(raised(array, jax.random.fold_in(stream_key, 3), *heavy), -bound, bound).astype(kind)


def setup_inputs(seed: int = 0) -> dict:
    splits = jax.random.split(jax.random.key(seed), 13)
    inputs = scatter_about(splits[0], (SEQS, LENGTH, MODEL_DIM), 1.0, 6.0, ((0, 4), (1, 8)))
    gain_one = jnp.clip(1.0 + 0.18 * jax.random.normal(splits[1], (MODEL_DIM,), jnp.float32), 0.099609375, 1.8984375).astype(jnp.bfloat16)
    query_weight = scatter_about(splits[2], (MODEL_DIM, QUERY_HEADS * HEAD_DIM), MODEL_DIM ** -0.5, 0.1875, ((0, 4), (1, 8)))
    key_weight = scatter_about(splits[3], (MODEL_DIM, KEY_VALUE_HEADS * HEAD_DIM), MODEL_DIM ** -0.5, 0.1875, ((0, 4), (1, 8)))
    value_weight = scatter_about(splits[4], (MODEL_DIM, KEY_VALUE_HEADS * HEAD_DIM), MODEL_DIM ** -0.5, 0.1875, ((0, 4), (1, 8)))
    output_weight = scatter_about(splits[5], (QUERY_HEADS * HEAD_DIM, MODEL_DIM), (QUERY_HEADS * HEAD_DIM // 64) ** -0.5, 1.5, ((0, 4), (1, 8)))
    gain_two = jnp.clip(1.0 + 0.18 * jax.random.normal(splits[6], (MODEL_DIM,), jnp.float32), 0.099609375, 1.8984375).astype(jnp.bfloat16)
    gate_weight = scatter_about(splits[7], (MODEL_DIM, FF), MODEL_DIM ** -0.5, 0.1875, ((0, 4), (1, 8)))
    up_weight = scatter_about(splits[8], (MODEL_DIM, FF), MODEL_DIM ** -0.5, 0.1875, ((0, 4), (1, 8)))
    down_weight = scatter_about(splits[9], (FF, MODEL_DIM), (FF // 4) ** -0.5, 0.25, ((0, 4), (1, 8)))
    segment_ids = jax.vmap(lambda own: jnp.searchsorted(jnp.cumsum(ragged_sizes(own, DOCS, LENGTH, DOC_MAX, 1)), jnp.arange(LENGTH), side="right"))(jax.random.split(splits[10], SEQS)).reshape((SEQS, LENGTH)).astype(jnp.int32)
    cotangent = gaussian_with(splits[11], (SEQS, LENGTH, MODEL_DIM), 1.0, 6.0, ((0, 4), (1, 8)), (1, 2, 8, 2.0))
    return dict(inputs=inputs, gain_one=gain_one, query_weight=query_weight, key_weight=key_weight, value_weight=value_weight, output_weight=output_weight, gain_two=gain_two, gate_weight=gate_weight, up_weight=up_weight, down_weight=down_weight, segment_ids=segment_ids, cotangent=cotangent)


@jax.custom_vjp
def lowered_dtype(v):
    return lax.optimization_barrier(v.astype(jnp.bfloat16)).astype(jnp.float32)

@jax.custom_vjp
def lowered_backward(v):
    return v

def low_keep(v):
    return (lowered_dtype(v), None)

def low_pass(kept, grad):
    return (grad,)

def back_keep(v):
    return (v, None)

def back_low(kept, grad):
    return (lowered_dtype(grad),)
lowered_dtype.defvjp(low_keep, low_pass)
lowered_backward.defvjp(back_keep, back_low)
epsilon = 1e-05
rope_base = 10000.0
masked = -1e+30
highest_precision = lax.Precision.HIGHEST

def rotate(values):
    half_width = values.shape[-1] // 2
    return jnp.concatenate([-values[..., half_width:], values[..., :half_width]], axis=-1)

def rope_tables(positions, head_width):
    freq_index = jnp.arange(head_width // 2, dtype=jnp.float32)
    frequency = jnp.exp(freq_index * (-2.0 * math.log(rope_base) / head_width))
    angles = positions[:, None] * frequency[None, :]
    angles = jnp.concatenate([angles, angles], axis=-1)
    return (jnp.cos(angles), jnp.sin(angles))

def rms_scale(values):
    return lax.rsqrt(lax.optimization_barrier(jnp.mean(values * values, axis=-1, keepdims=True)) + epsilon)

def attend(query_states, key_heads, value_heads, segment):
    query_group_width = QUERY_HEADS // KEY_VALUE_HEADS
    keys_wide = jnp.repeat(key_heads, query_group_width, axis=1)
    values_wide = jnp.repeat(value_heads, query_group_width, axis=1)
    sequence_length = query_states.shape[0]
    total_rows = 512 if sequence_length % 512 == 0 else sequence_length
    key_pos = jnp.arange(sequence_length, dtype=jnp.int32)
    score_scale = HEAD_DIM ** (-0.5)

    def query_block(first_row):
        query_rows = lax.dynamic_slice_in_dim(query_states, first_row, total_rows, 0)
        seg_rows = lax.dynamic_slice_in_dim(segment, first_row, total_rows, 0)
        query_pos = first_row + jnp.arange(total_rows, dtype=jnp.int32)
        raw_scores = jnp.einsum('qhd,khd->hqk', query_rows, keys_wide, precision=highest_precision)
        scores = lowered_backward(raw_scores * score_scale)
        allowed = (seg_rows[:, None] == segment[None, :]) & (query_pos[:, None] >= key_pos[None, :])
        scores = jnp.where(allowed[None], scores, masked)
        probs = jax.nn.softmax(scores, axis=-1)
        return jnp.einsum('hqk,khd->qhd', lowered_dtype(probs), values_wide, precision=highest_precision)
    starts = (jnp.arange(sequence_length // total_rows) * total_rows).astype(jnp.int32)
    blocks_out = lax.map(jax.checkpoint(query_block), starts)
    return blocks_out.reshape(sequence_length, QUERY_HEADS, HEAD_DIM)

def forward_layer(input_single, gain_one, query_weight, key_weight, value_weight, output_weight, gain_two, gate_weight, up_weight, down_weight, segment_ids):
    sequence_total, sequence_length, model_width = input_single.shape
    cosine_table, sine_values = rope_tables(jnp.arange(sequence_length, dtype=jnp.float32), HEAD_DIM)
    cosine_table = cosine_table[None, :, None, :]
    sine_values = sine_values[None, :, None, :]
    first_normed = lowered_dtype(input_single * rms_scale(input_single) * gain_one)
    query_states = lowered_backward(jnp.einsum('kwt,tf->kwf', first_normed, query_weight, precision=highest_precision)).reshape(sequence_total, sequence_length, QUERY_HEADS, HEAD_DIM)
    key_unrotated = lowered_backward(jnp.einsum('kwt,tf->kwf', first_normed, key_weight, precision=highest_precision)).reshape(sequence_total, sequence_length, KEY_VALUE_HEADS, HEAD_DIM)
    value_lowered = lowered_dtype(lowered_backward(jnp.einsum('kwt,tf->kwf', first_normed, value_weight, precision=highest_precision))).reshape(sequence_total, sequence_length, KEY_VALUE_HEADS, HEAD_DIM)
    query_rotated = lowered_dtype(query_states * cosine_table + rotate(query_states) * sine_values)
    key_rotated = lowered_dtype(key_unrotated * cosine_table + rotate(key_unrotated) * sine_values)
    heads = lax.map(lambda pieces: attend(pieces[0], pieces[1], pieces[2], pieces[3]), (query_rotated, key_rotated, value_lowered, segment_ids))
    attention_output = lowered_dtype(lowered_backward(heads.reshape(sequence_total, sequence_length, QUERY_HEADS * HEAD_DIM)))
    residual_state = input_single + lowered_backward(jnp.einsum('qpv,vj->qpj', attention_output, output_weight, precision=highest_precision))
    second_normed = lowered_dtype(residual_state * rms_scale(residual_state) * gain_two)
    gate_preactivation = lowered_backward(jnp.einsum('ray,yg->rag', second_normed, gate_weight, precision=highest_precision))
    up_preactivation = lowered_backward(jnp.einsum('ray,yg->rag', second_normed, up_weight, precision=highest_precision))
    hidden_state = lowered_dtype(jax.nn.silu(gate_preactivation) * up_preactivation)
    return residual_state + jnp.einsum('gjk,kq->gjq', hidden_state, down_weight, precision=highest_precision)

def reference(inputs, gain_one, query_weight, key_weight, value_weight, output_weight, gain_two, gate_weight, up_weight, down_weight, segment_ids, cotangent):
    floats = (inputs.astype(jnp.float32), gain_one.astype(jnp.float32), query_weight.astype(jnp.float32), key_weight.astype(jnp.float32), value_weight.astype(jnp.float32), output_weight.astype(jnp.float32), gain_two.astype(jnp.float32), gate_weight.astype(jnp.float32), up_weight.astype(jnp.float32), down_weight.astype(jnp.float32))

    def forward(input_single, g_one, m_query, m_key, m_value, m_out, g_two, m_gate, m_up, m_down):
        return forward_layer(input_single, g_one, m_query, m_key, m_value, m_out, g_two, m_gate, m_up, m_down, segment_ids)
    output, pullback = jax.vjp(forward, *floats)
    grads = pullback(cotangent.astype(jnp.float32))
    return (output.astype(jnp.bfloat16), grads[0].astype(jnp.bfloat16), grads[1], grads[2], grads[3], grads[4], grads[5], grads[6], grads[7], grads[8], grads[9])
```

```python
import functools
import math

import jax
import jax.numpy as jnp
from jax import lax
from jax.experimental import pallas as pl
from jax.experimental.pallas import tpu as pltpu
from jax.sharding import PartitionSpec as P

QUERY_HEADS = 15
KEY_VALUE_HEADS = 5
HEAD_DIM = 64
GROUP = QUERY_HEADS // KEY_VALUE_HEADS
HALF = HEAD_DIM // 2

epsilon = 1e-05
rope_base = 10000.0
masked = -1e30
f32 = jnp.float32
b16 = jnp.bfloat16


def bits_of(axis, size):
    masks = []
    mask = size // 2
    while mask:
        masks.append((axis, mask))
        mask //= 2
    return masks


def swap(values, axis, mask):
    size = lax.axis_size(axis)
    return lax.ppermute(values, axis, [(i, i ^ mask) for i in range(size)])


def bit(axis, mask):
    return (lax.axis_index(axis) // mask) % 2


def gather(block, order, major):
    rows, cols = block.shape
    have = []
    buf = block[None]
    for step in order:
        got = swap(buf, *step)
        before = [b for b in have if major.index(b) < major.index(step)]
        pre = 2 ** len(before)
        shape = (pre, buf.shape[0] // pre, rows, cols)
        mine, theirs = buf.reshape(shape), got.reshape(shape)
        upper = bit(*step) == 1
        buf = jnp.stack(
            [jnp.where(upper, theirs, mine), jnp.where(upper, mine, theirs)], axis=1
        ).reshape(-1, rows, cols)
        have.append(step)
    return buf


def scatter(buf, order, major):
    count, rows, cols = buf.shape
    have = list(major)
    for index, step in enumerate(order):
        pre = 2 ** have.index(step)
        shape = (pre, 2, buf.shape[0] // (2 * pre), rows, cols)
        parts = buf.reshape(shape)
        own = bit(*step)
        send = lax.dynamic_index_in_dim(parts, 1 - own, 1, keepdims=False)
        keep = lax.dynamic_index_in_dim(parts, own, 1, keepdims=False)
        got = swap(send, *step)
        buf = (keep.astype(f32) + got.astype(f32)).reshape(-1, rows, cols)
        if index < len(order) - 1:
            buf = buf.astype(b16)
        have.remove(step)
    return buf[0]


def shift_outer(values, by):
    size = lax.axis_size("ctx")
    return lax.ppermute(
        values, "ctx", [(i, i + 2 * by) for i in range(size) if 0 <= i + 2 * by < size]
    )


def dot(a, b, dims):
    return lax.dot_general(a, b, (dims, ((), ())), preferred_element_type=f32)


def fill_bias(blocks, tokens, place, seg_refs, bias):
    queries = jnp.broadcast_to(seg_refs[0][0:1, :].astype(f32), (tokens, tokens))
    for j in range(blocks):
        keys = jnp.broadcast_to(seg_refs[j][0:1, :].astype(f32), (tokens, tokens)).T
        allowed = (keys == queries) & (place >= j)
        if j == 0:
            key_row = lax.broadcasted_iota(jnp.int32, (tokens, tokens), 0)
            query_col = lax.broadcasted_iota(jnp.int32, (tokens, tokens), 1)
            allowed = allowed & (key_row <= query_col)
        bias[j * tokens : (j + 1) * tokens, :] = jnp.where(allowed, 0.0, masked)


def heads_side(ref):
    return jnp.concatenate(
        [ref[h * HEAD_DIM : (h + 1) * HEAD_DIM, :] for h in range(GROUP)], axis=1
    )


def forward_kernel(blocks, tokens, place_ref, *refs):
    q_ref = refs[0]
    k_refs = refs[1 : 1 + blocks]
    v_refs = refs[1 + blocks : 1 + 2 * blocks]
    seg_refs = refs[1 + 2 * blocks : 1 + 3 * blocks]
    att_ref, lse_ref, bias = refs[1 + 3 * blocks :]

    @pl.when(pl.program_id(1) == 0)
    def _():
        fill_bias(blocks, tokens, place_ref[0], seg_refs, bias)

    keys = jnp.concatenate([r[...] for r in k_refs], axis=1)
    values = jnp.concatenate([r[...] for r in v_refs], axis=1)
    scores = dot(keys, heads_side(q_ref), ((0,), (0,)))
    for h in range(GROUP):
        own = scores[:, h * tokens : (h + 1) * tokens] + bias[...]
        top = jnp.max(own, axis=0, keepdims=True)
        probs = jnp.exp(own - top)
        total = jnp.sum(probs, axis=0, keepdims=True)
        out = dot(values, probs.astype(b16), ((1,), (0,)))
        att_ref[h * HEAD_DIM : (h + 1) * HEAD_DIM, :] = (out / total).astype(b16)
        lse_ref[0, h : h + 1, :] = top + jnp.log(total)


def backward_kernel(blocks, tokens, place_ref, *refs):
    q_ref, datt_ref, lse_ref = refs[:3]
    k_refs = refs[3 : 3 + blocks]
    v_refs = refs[3 + blocks : 3 + 2 * blocks]
    seg_refs = refs[3 + 2 * blocks : 3 + 3 * blocks]
    dq_ref = refs[3 + 3 * blocks]
    dkv_refs = refs[4 + 3 * blocks : 4 + 4 * blocks]
    bias, p_scr, ds_scr = refs[4 + 4 * blocks :]

    @pl.when(pl.program_id(1) == 0)
    def _():
        fill_bias(blocks, tokens, place_ref[0], seg_refs, bias)

    keys = jnp.concatenate([r[...] for r in k_refs], axis=1)
    values = jnp.concatenate([r[...] for r in v_refs], axis=1)
    queries = heads_side(q_ref)
    grads = heads_side(datt_ref)
    scores = dot(keys, queries, ((0,), (0,)))
    d_probs = dot(values, grads, ((0,), (0,)))
    for h in range(GROUP):
        lanes = slice(h * tokens, (h + 1) * tokens)
        probs = jnp.exp(scores[:, lanes] + bias[...] - lse_ref[0, h : h + 1, :])
        weighted = probs * d_probs[:, lanes]
        delta = jnp.sum(weighted, axis=0, keepdims=True)
        p_scr[:, lanes] = probs.astype(b16)
        ds_scr[:, lanes] = (weighted - probs * delta).astype(b16)
    d_scores = ds_scr[...]
    dq = dot(keys, d_scores, ((1,), (0,)))
    for h in range(GROUP):
        dq_ref[h * HEAD_DIM : (h + 1) * HEAD_DIM, :] = dq[:, h * tokens : (h + 1) * tokens]
    dk = dot(queries, d_scores, ((1,), (1,)))
    dv = dot(grads, p_scr[...], ((1,), (1,)))
    for j in range(blocks):
        lanes = slice(j * tokens, (j + 1) * tokens)
        dkv_refs[j][0] = dk[:, lanes].astype(b16)
        dkv_refs[j][1] = dv[:, lanes].astype(b16)


def kv_specs(blocks, tokens):
    per_group = (HEAD_DIM, tokens)
    key = pl.BlockSpec(per_group, lambda s, g, _: (g, s))
    value = pl.BlockSpec(per_group, lambda s, g, _: (KEY_VALUE_HEADS + g, s))
    seg_row = 2 * KEY_VALUE_HEADS * HEAD_DIM // 16
    seg = pl.BlockSpec((16, tokens), lambda s, g, _: (seg_row, s))
    return [key] * blocks + [value] * blocks + [seg] * blocks


def attend(place, q_rot, pieces, sequences, tokens):
    blocks = len(pieces)
    heads = pl.BlockSpec((GROUP * HEAD_DIM, tokens), lambda s, g, _: (g, s))
    stat = pl.BlockSpec((1, 8, tokens), lambda s, g, _: (g, 0, s))
    wide = sequences * tokens
    return pl.pallas_call(
        functools.partial(forward_kernel, blocks, tokens),
        grid_spec=pltpu.PrefetchScalarGridSpec(
            num_scalar_prefetch=1,
            grid=(sequences, KEY_VALUE_HEADS),
            in_specs=[heads] + kv_specs(blocks, tokens),
            out_specs=[heads, stat],
            scratch_shapes=[pltpu.VMEM((blocks * tokens, tokens), f32)],
        ),
        out_shape=[
            jax.ShapeDtypeStruct((QUERY_HEADS * HEAD_DIM, wide), b16),
            jax.ShapeDtypeStruct((KEY_VALUE_HEADS, 8, wide), f32),
        ],
        compiler_params=pltpu.CompilerParams(vmem_limit_bytes=40 << 20),
        name="attend",
    )(place, q_rot, *pieces, *pieces, *pieces)


def attend_back(place, q_rot, datt, lse, pieces, sequences, tokens):
    blocks = len(pieces)
    heads = pl.BlockSpec((GROUP * HEAD_DIM, tokens), lambda s, g, _: (g, s))
    stat = pl.BlockSpec((1, 8, tokens), lambda s, g, _: (g, 0, s))
    pair = pl.BlockSpec((2, HEAD_DIM, tokens), lambda s, g, _: (0, g, s))
    wide = sequences * tokens
    return pl.pallas_call(
        functools.partial(backward_kernel, blocks, tokens),
        grid_spec=pltpu.PrefetchScalarGridSpec(
            num_scalar_prefetch=1,
            grid=(sequences, KEY_VALUE_HEADS),
            in_specs=[heads, heads, stat] + kv_specs(blocks, tokens),
            out_specs=[heads] + [pair] * blocks,
            scratch_shapes=[
                pltpu.VMEM((blocks * tokens, tokens), f32),
                pltpu.VMEM((blocks * tokens, GROUP * tokens), b16),
                pltpu.VMEM((blocks * tokens, GROUP * tokens), b16),
            ],
        ),
        out_shape=[jax.ShapeDtypeStruct((QUERY_HEADS * HEAD_DIM, wide), f32)]
        + [jax.ShapeDtypeStruct((2, KEY_VALUE_HEADS * HEAD_DIM, wide), b16)] * blocks,
        compiler_params=pltpu.CompilerParams(vmem_limit_bytes=48 << 20),
        name="attend_back",
    )(place, q_rot, datt, lse, *pieces, *pieces, *pieces)


def per_device(
    inputs,
    gain_one,
    query_weight,
    key_weight,
    value_weight,
    output_weight,
    gain_two,
    gate_weight,
    up_weight,
    down_weight,
    segment_ids,
    cotangent,
):
    dp, ctx = lax.axis_size("dp"), lax.axis_size("ctx")
    sequences, tokens, width = inputs.shape
    total = sequences * tokens
    rows = query_weight.shape[0]
    q_cols, kv_cols = query_weight.shape[1], key_weight.shape[1]
    ff_cols = gate_weight.shape[1]
    ff = ff_cols * ctx
    down_rows, out_cols = down_weight.shape
    kv_width = KEY_VALUE_HEADS * HEAD_DIM

    dp_bits, ctx_bits = bits_of("dp", dp), bits_of("ctx", ctx)
    dp_major = dp_bits + ctx_bits
    ctx_major = ctx_bits + dp_bits
    x_last = ctx_bits + dp_bits
    y_last = ctx_bits[:-1] + dp_bits[:-1] + ctx_bits[-1:] + dp_bits[-1:]

    place = lax.axis_index("ctx")

    gains = jnp.stack([gain_one, gain_two])
    gain_rows = -(-gains.size // rows)
    gains = jnp.pad(gains.reshape(-1), (0, gain_rows * rows - gains.size)).reshape(gain_rows, rows)
    pad_rows = -(q_cols + 2 * kv_cols + gain_rows) % 16
    qkv_block = jnp.concatenate(
        [query_weight.T, key_weight.T, value_weight.T, gains, jnp.zeros((pad_rows, rows), b16)]
    )
    qkv_all = gather(qkv_block, y_last, dp_major).reshape(dp, ctx, -1, rows)
    out_all = gather(output_weight.T, x_last, dp_major).reshape(dp, ctx, -1, rows)
    gu_all = gather(jnp.concatenate([gate_weight, up_weight], axis=1), x_last, ctx_major).reshape(
        ctx, dp, rows, 2 * ff_cols
    )
    down_all = gather(down_weight.T, y_last, dp_major).reshape(dp, ctx, out_cols, down_rows)

    def columns(piece):
        return jnp.transpose(piece, (1, 2, 0, 3)).reshape(-1, dp * rows)

    wq = columns(qkv_all[:, :, :q_cols])
    wk = columns(qkv_all[:, :, q_cols : q_cols + kv_cols])
    wv = columns(qkv_all[:, :, q_cols + kv_cols : q_cols + 2 * kv_cols])
    w_qkv = jnp.concatenate([wq, wk, wv])
    first_gain = q_cols + 2 * kv_cols
    gain_all = qkv_all[0, :, first_gain : first_gain + gain_rows].reshape(ctx, -1)
    gain_part = gain_one.shape[0]
    gain_a = gain_all[:, :gain_part].reshape(width).astype(f32)
    gain_b = gain_all[:, gain_part : 2 * gain_part].reshape(width).astype(f32)
    wo = columns(out_all)

    x = inputs.reshape(total, width).astype(f32)
    inv_one = lax.rsqrt(jnp.mean(x * x, axis=-1, keepdims=True) + epsilon)
    normed_one = (x * inv_one * gain_a).astype(b16)
    qkv = dot(w_qkv, normed_one, ((1,), (1,)))
    positions = (place * tokens + jnp.arange(tokens, dtype=jnp.int32)).astype(f32)
    positions = jnp.tile(positions, sequences)
    frequency = jnp.exp(jnp.arange(HALF, dtype=f32) * (-2.0 * math.log(rope_base) / HEAD_DIM))
    angles = frequency[:, None] * positions[None, :]
    cosine, sine = jnp.cos(angles), jnp.sin(angles)

    def turn(values, sign):
        parts = values.reshape(-1, 2, HALF, total)
        low, high = parts[:, 0], parts[:, 1]
        return jnp.stack(
            [low * cosine - sign * high * sine, high * cosine + sign * low * sine], axis=1
        ).reshape(-1, total)

    score_scale = HEAD_DIM ** (-0.5)
    q_rot = (turn(qkv[:width], 1.0) * score_scale).astype(b16)
    k_rot = turn(qkv[width : width + kv_width], 1.0).astype(b16)
    v_low = qkv[width + kv_width :].astype(b16)
    seg_row = jnp.pad(segment_ids.reshape(1, total).astype(b16), ((0, 15), (0, 0)))
    own = jnp.concatenate([k_rot, v_low, seg_row])

    steps = ctx // 4
    inner = bit("ctx", 1)
    straight = [own]
    for _ in range(steps):
        straight.append(shift_outer(straight[-1], 1))
    crossed = [
        swap(jnp.where(inner == 0, straight[k], straight[k + 1]), "ctx", 1) for k in range(steps)
    ]
    pieces = []
    for k in range(steps):
        pieces += [straight[k], crossed[k]]
    pieces.append(straight[steps])

    place_arg = place.reshape(1).astype(jnp.int32)
    att, lse = attend(place_arg, q_rot, pieces, sequences, tokens)

    mid = x + dot(att, wo, ((0,), (1,)))
    inv_two = lax.rsqrt(jnp.mean(mid * mid, axis=-1, keepdims=True) + epsilon)
    normed_two = (mid * inv_two * gain_b).astype(b16)
    w_gate = jnp.transpose(gu_all[..., :ff_cols], (1, 2, 0, 3)).reshape(width, ff)
    w_up = jnp.transpose(gu_all[..., ff_cols:], (1, 2, 0, 3)).reshape(width, ff)
    w_down = jnp.transpose(down_all, (1, 2, 0, 3)).reshape(width, ff)
    gate = dot(normed_two, w_gate, ((1,), (0,)))
    up = dot(normed_two, w_up, ((1,), (0,)))
    sigma = jax.nn.sigmoid(gate)
    hidden = (gate * sigma * up).astype(b16)
    output = (mid + dot(hidden, w_down, ((1,), (1,)))).astype(b16)

    cot = cotangent.reshape(total, width)
    d_hidden = dot(cot, w_down, ((1,), (0,)))
    d_up = (d_hidden * gate * sigma).astype(b16)
    d_gate = (d_hidden * up * sigma * (1.0 + gate * (1.0 - sigma))).astype(b16)
    g_down = dot(cot, hidden, ((0,), (0,))).astype(b16)
    g_down = jnp.transpose(g_down.reshape(ctx, out_cols, dp, down_rows), (2, 0, 1, 3))
    g_down = scatter(
        g_down.reshape(dp * ctx, out_cols, down_rows), y_last[::-1], dp_major
    )
    g_gate = dot(normed_two, d_gate, ((0,), (0,))).astype(b16)
    g_up = dot(normed_two, d_up, ((0,), (0,))).astype(b16)
    g_gu = jnp.concatenate(
        [
            jnp.transpose(g.reshape(dp, rows, ctx, ff_cols), (2, 0, 1, 3))
            for g in (g_gate, g_up)
        ],
        axis=-1,
    )
    g_gu = scatter(g_gu.reshape(ctx * dp, rows, 2 * ff_cols), x_last[::-1], ctx_major)
    d_normed_two = dot(d_gate, w_gate, ((1,), (1,))) + dot(d_up, w_up, ((1,), (1,)))
    g_gain_two = jnp.sum(d_normed_two * mid * inv_two, axis=0)
    scaled_two = gain_b * d_normed_two
    d_mid = (
        cot.astype(f32)
        + inv_two * scaled_two
        - mid * inv_two**3 * jnp.mean(scaled_two * mid, axis=-1, keepdims=True)
    )
    d_mid_low = d_mid.astype(b16)

    def to_blocks(grad, n):
        return jnp.transpose(grad.reshape(ctx, n, dp, rows), (2, 0, 1, 3))

    g_out = dot(d_mid_low, att, ((0,), (1,))).astype(b16)
    g_out = scatter(
        to_blocks(g_out, out_cols).reshape(dp * ctx, out_cols, rows), x_last[::-1], dp_major
    )
    d_att = dot(wo, d_mid_low, ((0,), (1,))).astype(b16)
    dq_rot, *parts = attend_back(place_arg, q_rot, d_att, lse, pieces, sequences, tokens)

    returned = [swap(parts[2 * k + 1], "ctx", 1).astype(f32) for k in range(steps)]
    here = []
    for k in range(steps + 1):
        value = parts[2 * k].astype(f32)
        if k < steps:
            value = value + jnp.where(inner == 0, returned[k], 0.0)
        if k > 0:
            value = value + jnp.where(inner == 1, returned[k - 1], 0.0)
        here.append(value)
    carried = here[steps]
    for k in range(steps, 0, -1):
        carried = here[k - 1] + shift_outer(carried.astype(b16), -1).astype(f32)

    d_q = (turn(dq_rot, -1.0) * score_scale).astype(b16)
    d_k = turn(carried[0], -1.0).astype(b16)
    d_v = carried[1].astype(b16)
    d_qkv = jnp.concatenate([d_q, d_k, d_v])
    g_qkv = dot(d_qkv, normed_one, ((1,), (0,))).astype(b16)
    d_normed_one = dot(d_qkv, w_qkv, ((0,), (0,)))
    g_gain_one = jnp.sum(d_normed_one * x * inv_one, axis=0)
    scaled_one = gain_a * d_normed_one
    input_grad = (
        d_mid
        + inv_one * scaled_one
        - x * inv_one**3 * jnp.mean(scaled_one * x, axis=-1, keepdims=True)
    ).astype(b16)

    g_gains = jnp.concatenate(
        [g_gain_one.reshape(ctx, gain_part), g_gain_two.reshape(ctx, gain_part)], axis=1
    ).astype(b16)
    g_gains = jnp.pad(g_gains, ((0, 0), (0, gain_rows * rows - 2 * gain_part)))
    g_gains = jnp.broadcast_to(g_gains.reshape(1, ctx, gain_rows, rows), (dp, ctx, gain_rows, rows))
    g_block = jnp.concatenate(
        [
            to_blocks(g_qkv[:width], q_cols),
            to_blocks(g_qkv[width : width + kv_width], kv_cols),
            to_blocks(g_qkv[width + kv_width :], kv_cols),
            g_gains,
            jnp.zeros((dp, ctx, pad_rows, rows), b16),
        ],
        axis=2,
    )
    g_block = scatter(g_block.reshape(dp * ctx, -1, rows), y_last[::-1], dp_major)
    g_gains = g_block[first_gain : first_gain + gain_rows].reshape(-1)
    return (
        output.reshape(sequences, tokens, width),
        input_grad.reshape(sequences, tokens, width),
        g_gains[:gain_part],
        g_block[:q_cols].T,
        g_block[q_cols : q_cols + kv_cols].T,
        g_block[q_cols + kv_cols : first_gain].T,
        g_out.T,
        g_gains[gain_part : 2 * gain_part],
        g_gu[:, :ff_cols],
        g_gu[:, ff_cols:],
        g_down.T,
    )


def solution(mesh):
    act = P("dp", "ctx", None)
    weight = P("dp", "ctx")
    gain = P("ctx")
    return jax.shard_map(
        per_device,
        mesh=mesh,
        in_specs=(
            act, gain, weight, weight, weight, weight, gain, weight, weight, weight, P("dp", "ctx"), act,
        ),
        out_specs=(
            act, act, gain, weight, weight, weight, weight, gain, weight, weight, weight,
        ),
        check_vma=False,
    )
```

```python
import functools
import math

import jax
import jax.numpy as jnp
from jax import lax
from jax.experimental import pallas as pl
from jax.experimental.pallas import tpu as pltpu
from jax.sharding import PartitionSpec as P

QUERY_HEADS = 15
KEY_VALUE_HEADS = 5
HEAD_DIM = 64
GROUP = QUERY_HEADS // KEY_VALUE_HEADS
HALF = HEAD_DIM // 2

epsilon = 1e-05
rope_base = 10000.0
masked = -1e30
f32 = jnp.float32
b16 = jnp.bfloat16


def bits_of(axis, size):
    masks = []
    mask = size // 2
    while mask:
        masks.append((axis, mask))
        mask //= 2
    return masks


def swap(values, axis, mask):
    size = lax.axis_size(axis)
    return lax.ppermute(values, axis, [(i, i ^ mask) for i in range(size)])


def bit(axis, mask):
    return (lax.axis_index(axis) // mask) % 2


def gather(block, order):
    bufs = [block[None]]
    for index, (axis, mask) in enumerate(order):
        got = [swap(b, axis, mask) for b in bufs]
        if axis == "dp":
            bufs = bufs + got
            continue
        upper = bit(axis, mask) == 1
        pre = 1
        for earlier in order[:index]:
            pre *= 2 if earlier[0] == "ctx" else 1
        merged = []
        for mine, theirs in zip(bufs, got, strict=True):
            shape = (pre, 1) + mine.shape[1:]
            mine, theirs = mine.reshape(shape), theirs.reshape(shape)
            both = jnp.concatenate(
                [jnp.where(upper, theirs, mine), jnp.where(upper, mine, theirs)], axis=1
            )
            merged.append(both.reshape((2 * pre,) + shape[2:]))
        bufs = merged
    dp_masks = [mask for axis, mask in order if axis == "dp"]
    out = [None] * len(bufs)
    for i, b in enumerate(bufs):
        out[sum(m for j, m in enumerate(dp_masks) if (i >> j) & 1)] = b
    return out


def scatter(bufs, order):
    bufs = dict(enumerate(bufs))
    for index, (axis, mask) in enumerate(order):
        last = index == len(order) - 1
        if axis == "dp":
            keep = {r: b for r, b in bufs.items() if not r & mask}
            send = {r: bufs[r ^ mask] for r in keep}
        else:
            own = bit(axis, mask)
            keep, send = {}, {}
            for r, b in bufs.items():
                parts = b.reshape((b.shape[0] // 2, 2) + b.shape[1:])
                send[r] = lax.dynamic_index_in_dim(parts, 1 - own, 1, keepdims=False)
                keep[r] = lax.dynamic_index_in_dim(parts, own, 1, keepdims=False)
        bufs = {}
        for r in keep:
            total = keep[r].astype(f32) + swap(send[r], axis, mask).astype(f32)
            bufs[r] = total if last else total.astype(b16)
    return bufs[0][0]


def sum_everywhere(values, bits):
    for axis, mask in bits:
        values = values + swap(values, axis, mask)
    return values


def shift_outer(values, by):
    size = lax.axis_size("ctx")
    return lax.ppermute(
        values, "ctx", [(i, i + 2 * by) for i in range(size) if 0 <= i + 2 * by < size]
    )


def dot(a, b, dims):
    return lax.dot_general(a, b, (dims, ((), ())), preferred_element_type=f32)


def fill_bias(blocks, tokens, place, seg_refs, bias):
    queries = jnp.broadcast_to(seg_refs[0][0:1, :].astype(f32), (tokens, tokens))
    for j in range(blocks):
        keys = jnp.broadcast_to(seg_refs[j][0:1, :].astype(f32), (tokens, tokens)).T
        allowed = (keys == queries) & (place >= j)
        if j == 0:
            key_row = lax.broadcasted_iota(jnp.int32, (tokens, tokens), 0)
            query_col = lax.broadcasted_iota(jnp.int32, (tokens, tokens), 1)
            allowed = allowed & (key_row <= query_col)
        bias[j * tokens : (j + 1) * tokens, :] = jnp.where(allowed, 0.0, masked)


def heads_side(ref):
    return jnp.concatenate(
        [ref[h * HEAD_DIM : (h + 1) * HEAD_DIM, :] for h in range(GROUP)], axis=1
    )


def forward_kernel(blocks, tokens, place_ref, *refs):
    q_ref = refs[0]
    k_refs = refs[1 : 1 + blocks]
    v_refs = refs[1 + blocks : 1 + 2 * blocks]
    seg_refs = refs[1 + 2 * blocks : 1 + 3 * blocks]
    att_ref, lse_ref, bias = refs[1 + 3 * blocks :]

    @pl.when(pl.program_id(1) == 0)
    def _():
        fill_bias(blocks, tokens, place_ref[0], seg_refs, bias)

    keys = jnp.concatenate([r[...] for r in k_refs], axis=1)
    values = jnp.concatenate([r[...] for r in v_refs], axis=1)
    scores = dot(keys, heads_side(q_ref), ((0,), (0,)))
    for h in range(GROUP):
        own = scores[:, h * tokens : (h + 1) * tokens] + bias[...]
        top = jnp.max(own, axis=0, keepdims=True)
        probs = jnp.exp(own - top)
        total = jnp.sum(probs, axis=0, keepdims=True)
        out = dot(values, probs.astype(b16), ((1,), (0,)))
        att_ref[h * HEAD_DIM : (h + 1) * HEAD_DIM, :] = (out / total).astype(b16)
        lse_ref[0, h : h + 1, :] = top + jnp.log(total)


def backward_kernel(blocks, tokens, place_ref, *refs):
    q_ref, datt_ref, lse_ref = refs[:3]
    k_refs = refs[3 : 3 + blocks]
    v_refs = refs[3 + blocks : 3 + 2 * blocks]
    seg_refs = refs[3 + 2 * blocks : 3 + 3 * blocks]
    dq_ref = refs[3 + 3 * blocks]
    dkv_refs = refs[4 + 3 * blocks : 4 + 4 * blocks]
    bias, p_scr, ds_scr = refs[4 + 4 * blocks :]

    @pl.when(pl.program_id(1) == 0)
    def _():
        fill_bias(blocks, tokens, place_ref[0], seg_refs, bias)

    keys = jnp.concatenate([r[...] for r in k_refs], axis=1)
    values = jnp.concatenate([r[...] for r in v_refs], axis=1)
    queries = heads_side(q_ref)
    grads = heads_side(datt_ref)
    scores = dot(keys, queries, ((0,), (0,)))
    d_probs = dot(values, grads, ((0,), (0,)))
    for h in range(GROUP):
        lanes = slice(h * tokens, (h + 1) * tokens)
        probs = jnp.exp(scores[:, lanes] + bias[...] - lse_ref[0, h : h + 1, :])
        weighted = probs * d_probs[:, lanes]
        delta = jnp.sum(weighted, axis=0, keepdims=True)
        p_scr[:, lanes] = probs.astype(b16)
        ds_scr[:, lanes] = (weighted - probs * delta).astype(b16)
    d_scores = ds_scr[...]
    dq = dot(keys, d_scores, ((1,), (0,)))
    for h in range(GROUP):
        dq_ref[h * HEAD_DIM : (h + 1) * HEAD_DIM, :] = dq[:, h * tokens : (h + 1) * tokens]
    dk = dot(queries, d_scores, ((1,), (1,)))
    dv = dot(grads, p_scr[...], ((1,), (1,)))
    for j in range(blocks):
        lanes = slice(j * tokens, (j + 1) * tokens)
        dkv_refs[j][0] = dk[:, lanes].astype(b16)
        dkv_refs[j][1] = dv[:, lanes].astype(b16)


def kv_specs(blocks, tokens):
    per_group = (HEAD_DIM, tokens)
    key = pl.BlockSpec(per_group, lambda s, g, _: (g, s))
    value = pl.BlockSpec(per_group, lambda s, g, _: (KEY_VALUE_HEADS + g, s))
    seg_row = 2 * KEY_VALUE_HEADS * HEAD_DIM // 16
    seg = pl.BlockSpec((16, tokens), lambda s, g, _: (seg_row, s))
    return [key] * blocks + [value] * blocks + [seg] * blocks


def attend(place, q_rot, pieces, sequences, tokens):
    blocks = len(pieces)
    heads = pl.BlockSpec((GROUP * HEAD_DIM, tokens), lambda s, g, _: (g, s))
    stat = pl.BlockSpec((1, 8, tokens), lambda s, g, _: (g, 0, s))
    wide = sequences * tokens
    return pl.pallas_call(
        functools.partial(forward_kernel, blocks, tokens),
        grid_spec=pltpu.PrefetchScalarGridSpec(
            num_scalar_prefetch=1,
            grid=(sequences, KEY_VALUE_HEADS),
            in_specs=[heads] + kv_specs(blocks, tokens),
            out_specs=[heads, stat],
            scratch_shapes=[pltpu.VMEM((blocks * tokens, tokens), f32)],
        ),
        out_shape=[
            jax.ShapeDtypeStruct((QUERY_HEADS * HEAD_DIM, wide), b16),
            jax.ShapeDtypeStruct((KEY_VALUE_HEADS, 8, wide), f32),
        ],
        compiler_params=pltpu.CompilerParams(vmem_limit_bytes=40 << 20),
        name="attend",
    )(place, q_rot, *pieces, *pieces, *pieces)


def attend_back(place, q_rot, datt, lse, pieces, sequences, tokens):
    blocks = len(pieces)
    heads = pl.BlockSpec((GROUP * HEAD_DIM, tokens), lambda s, g, _: (g, s))
    stat = pl.BlockSpec((1, 8, tokens), lambda s, g, _: (g, 0, s))
    pair = pl.BlockSpec((2, HEAD_DIM, tokens), lambda s, g, _: (0, g, s))
    wide = sequences * tokens
    return pl.pallas_call(
        functools.partial(backward_kernel, blocks, tokens),
        grid_spec=pltpu.PrefetchScalarGridSpec(
            num_scalar_prefetch=1,
            grid=(sequences, KEY_VALUE_HEADS),
            in_specs=[heads, heads, stat] + kv_specs(blocks, tokens),
            out_specs=[heads] + [pair] * blocks,
            scratch_shapes=[
                pltpu.VMEM((blocks * tokens, tokens), f32),
                pltpu.VMEM((blocks * tokens, GROUP * tokens), b16),
                pltpu.VMEM((blocks * tokens, GROUP * tokens), b16),
            ],
        ),
        out_shape=[jax.ShapeDtypeStruct((QUERY_HEADS * HEAD_DIM, wide), f32)]
        + [jax.ShapeDtypeStruct((2, KEY_VALUE_HEADS * HEAD_DIM, wide), b16)] * blocks,
        compiler_params=pltpu.CompilerParams(vmem_limit_bytes=48 << 20),
        name="attend_back",
    )(place, q_rot, datt, lse, *pieces, *pieces, *pieces)


def turned(low, high, cosine, sine, sign):
    return low * cosine - sign * high * sine, high * cosine + sign * low * sine


def project_kernel(parts, q_cols, kv_cols, ctx, scale, *refs):
    n_ref = refs[0]
    w_refs = refs[1 : 1 + parts]
    seg_ref, cos_ref, sin_ref, q_ref, own_ref, blocks, flat = refs[1 + parts :]
    acc = dot(w_refs[0][...], n_ref[0], ((1,), (0,)))
    for r in range(1, parts):
        acc = acc + dot(w_refs[r][...], n_ref[r], ((1,), (0,)))
    blocks[...] = acc
    rows = blocks.shape[0] // ctx
    width, kv_width = QUERY_HEADS * HEAD_DIM, KEY_VALUE_HEADS * HEAD_DIM
    for c in range(ctx):
        base = c * rows
        flat[c * q_cols : (c + 1) * q_cols] = blocks[base : base + q_cols]
        base += q_cols
        at = width + c * kv_cols
        flat[at : at + kv_cols] = blocks[base : base + kv_cols]
        base += kv_cols
        at += kv_width
        flat[at : at + kv_cols] = blocks[base : base + kv_cols]
    cosine, sine = cos_ref[...], sin_ref[...]
    for h in range(QUERY_HEADS + KEY_VALUE_HEADS):
        at = h * HEAD_DIM
        pair = turned(flat[at : at + HALF], flat[at + HALF : at + HEAD_DIM], cosine, sine, 1.0)
        for i, half in enumerate(pair):
            if h < QUERY_HEADS:
                q_ref[at + i * HALF : at + (i + 1) * HALF] = (half * scale).astype(b16)
            else:
                to = at - width + i * HALF
                own_ref[to : to + HALF] = half.astype(b16)
    own_ref[kv_width : 2 * kv_width] = flat[width + kv_width : width + 2 * kv_width].astype(b16)
    own_ref[2 * kv_width : 2 * kv_width + 16] = seg_ref[...]


def project_back_kernel(parts, q_cols, kv_cols, ctx, scale, *refs):
    dq_ref, dkv_ref, cos_ref, sin_ref, n_ref = refs[:5]
    w_refs = refs[5 : 5 + parts]
    dn_ref = refs[5 + parts]
    g_refs = refs[6 + parts : 6 + 2 * parts]
    flat, blocks = refs[6 + 2 * parts :]
    cosine, sine = cos_ref[...], sin_ref[...]
    width, kv_width = QUERY_HEADS * HEAD_DIM, KEY_VALUE_HEADS * HEAD_DIM
    for h in range(QUERY_HEADS + KEY_VALUE_HEADS):
        at = h * HEAD_DIM
        if h < QUERY_HEADS:
            low, high = dq_ref[at : at + HALF] * scale, dq_ref[at + HALF : at + HEAD_DIM] * scale
        else:
            to = at - width
            low, high = dkv_ref[0, to : to + HALF], dkv_ref[0, to + HALF : to + HEAD_DIM]
        pair = turned(low, high, cosine, sine, -1.0)
        for i, half in enumerate(pair):
            flat[at + i * HALF : at + (i + 1) * HALF] = half
    flat[width + kv_width : width + 2 * kv_width] = dkv_ref[1]
    rows = blocks.shape[0] // ctx
    tail = rows - q_cols - 2 * kv_cols
    for c in range(ctx):
        at = width + c * kv_cols
        pieces = [
            flat[c * q_cols : (c + 1) * q_cols],
            flat[at : at + kv_cols],
            flat[at + kv_width : at + kv_width + kv_cols],
            jnp.zeros((tail, flat.shape[1]), f32),
        ]
        blocks[c * rows : (c + 1) * rows] = jnp.concatenate(pieces, axis=0).astype(b16)
    for r in range(parts):
        g_refs[r][...] = dot(blocks[...], n_ref[r], ((1,), (1,))).astype(b16)
        dn_ref[r] = dot(w_refs[r][...], blocks[...], ((0,), (0,)))


def mix_kernel(parts, me_ref, att_ref, x_ref, gain_ref, *refs):
    w_refs = refs[:parts]
    mid_ref, inv_ref, normed_ref = refs[parts:]
    mid = x_ref[...].astype(f32)
    for r in range(parts):
        mid = mid + dot(att_ref[me_ref[0] ^ r], w_refs[r][...], ((0,), (1,)))
    mid_ref[...] = mid
    inv = lax.rsqrt(jnp.mean(mid * mid, axis=-1, keepdims=True) + epsilon)
    inv_ref[...] = inv
    normed_ref[...] = (mid * inv * gain_ref[...]).astype(b16)


def mix_back_kernel(parts, me_ref, att_ref, grad_ref, *refs):
    w_refs = refs[:parts]
    datt_ref = refs[parts]
    g_refs = refs[1 + parts :]
    flipped = grad_ref[...].T.astype(b16)
    for r in range(parts):
        at = me_ref[0] ^ r
        g_refs[r][...] = dot(flipped, att_ref[at], ((1,), (1,))).astype(b16)
        datt_ref[at] = dot(w_refs[r][...], flipped, ((0,), (0,))).astype(b16)


def ffn_kernel(parts, per, me_ref, n_ref, nt_ref, cot_ref, cot_t_ref, mid_ref, *refs):
    f_refs = refs[:parts]
    d_refs = refs[parts : 2 * parts]
    out_ref, dn_ref = refs[2 * parts : 2 * parts + 2]
    gf_refs = refs[2 * parts + 2 : 3 * parts + 2]
    gd_refs = refs[3 * parts + 2 : 4 * parts + 2]
    acc, down, g_down, hidden = refs[4 * parts + 2 :]
    step = pl.program_id(0)
    for r in range(parts):

        @pl.when(step == r)
        def _(r=r):
            down[...] = d_refs[r][...]

    @pl.when(step == 0)
    def _():
        acc[...] = jnp.zeros_like(acc)
        dn_ref[...] = jnp.zeros_like(dn_ref)

    ff = f_refs[0].shape[2] // 2
    d_hidden = dot(cot_ref[...], down[...], ((1,), (0,)))
    for i in range(per):
        both = dot(n_ref[0], f_refs[0][i], ((1,), (0,)))
        for r in range(1, parts):
            both = both + dot(n_ref[r], f_refs[r][i], ((1,), (0,)))
        gate, up = both[:, :ff], both[:, ff:]
        grad = d_hidden[:, i * ff : (i + 1) * ff]
        sigma = jax.nn.sigmoid(gate)
        silu = gate * sigma
        hidden[:, i * ff : (i + 1) * ff] = (silu * up).astype(b16)
        d_gate = grad * up * (sigma * (1.0 + gate * (1.0 - sigma)))
        d_both = jnp.concatenate([d_gate, grad * silu], axis=1).astype(b16)
        for r in range(parts):
            gf_refs[r][i] = dot(nt_ref[r], d_both, ((1,), (0,))).astype(b16)
            dn_ref[r] += dot(d_both, f_refs[r][i], ((1,), (1,)))
    acc[...] += dot(hidden[...], down[...], ((1,), (1,)))
    g_down[...] = dot(cot_t_ref[...], hidden[...], ((1,), (0,))).astype(b16)
    for r in range(parts):

        @pl.when(step == r)
        def _(r=r):
            gd_refs[r][...] = g_down[...]

    @pl.when(step == parts - 1)
    def _():
        out_ref[...] = (mid_ref[...] + acc[...]).astype(b16)


def ffn(me, n_rel, nt_rel, cot, cot_t, mid, f_list, d_list):
    parts = len(f_list)
    ctx, rows, wide = f_list[0].shape
    per = ctx // parts
    tokens, width = mid.shape
    down_shape = d_list[0].shape

    def whole(a):
        return pl.BlockSpec(a.shape, lambda i, me: (0,) * a.ndim, pipeline_mode=pl.Buffered(1))

    f_spec = pl.BlockSpec((per, rows, wide), lambda i, me: (me[0] ^ i, 0, 0))
    out_shape = [
        jax.ShapeDtypeStruct((tokens, width), b16),
        jax.ShapeDtypeStruct((parts, tokens, rows), f32),
    ]
    out_shape += [jax.ShapeDtypeStruct((ctx, rows, wide), b16)] * parts
    out_shape += [jax.ShapeDtypeStruct(down_shape, b16)] * parts
    return pl.pallas_call(
        functools.partial(ffn_kernel, parts, per),
        grid_spec=pltpu.PrefetchScalarGridSpec(
            num_scalar_prefetch=1,
            grid=(parts,),
            in_specs=[whole(a) for a in (n_rel, nt_rel, cot, cot_t, mid)]
            + [f_spec] * parts
            + [whole(a) for a in d_list],
            out_specs=[whole(a) for a in out_shape[:2]]
            + [f_spec] * parts
            + [whole(a) for a in d_list],
            scratch_shapes=[
                pltpu.VMEM((tokens, width), f32),
                pltpu.VMEM(down_shape, b16),
                pltpu.VMEM(down_shape, b16),
                pltpu.VMEM((tokens, per * wide // 2), b16),
            ],
        ),
        out_shape=out_shape,
        compiler_params=pltpu.CompilerParams(vmem_limit_bytes=58 << 20),
        name="ffn",
    )(me, n_rel, nt_rel, cot, cot_t, mid, *f_list, *d_list)


def in_vmem(kernel, name, out_shape, scratch, *args, scalars=0):
    vmem = pl.BlockSpec(memory_space=pltpu.VMEM)
    smem = pl.BlockSpec(memory_space=pltpu.SMEM)
    return pl.pallas_call(
        kernel,
        in_specs=[smem] * scalars + [vmem] * (len(args) - scalars),
        out_specs=[vmem] * len(out_shape),
        out_shape=out_shape,
        scratch_shapes=scratch,
        compiler_params=pltpu.CompilerParams(vmem_limit_bytes=48 << 20),
        name=name,
    )(*args)


def per_device(
    inputs,
    gain_one,
    query_weight,
    key_weight,
    value_weight,
    output_weight,
    gain_two,
    gate_weight,
    up_weight,
    down_weight,
    segment_ids,
    cotangent,
):
    dp, ctx = lax.axis_size("dp"), lax.axis_size("ctx")
    sequences, tokens, width = inputs.shape
    total = sequences * tokens
    rows = query_weight.shape[0]
    q_cols, kv_cols = query_weight.shape[1], key_weight.shape[1]
    ff_cols = gate_weight.shape[1]
    down_rows, out_cols = down_weight.shape
    kv_width = KEY_VALUE_HEADS * HEAD_DIM
    shape_of = jax.ShapeDtypeStruct

    dp_bits, ctx_bits = bits_of("dp", dp), bits_of("ctx", ctx)
    x_last = ctx_bits + dp_bits
    y_last = ctx_bits[:-1] + dp_bits[:-1] + ctx_bits[-1:] + dp_bits[-1:]

    place = lax.axis_index("ctx")
    me = lax.axis_index("dp")
    me_arg = me.reshape(1).astype(jnp.int32)
    place_arg = place.reshape(1).astype(jnp.int32)

    def relative(stacked):
        return jnp.stack(
            [lax.dynamic_index_in_dim(stacked, me ^ r, 0, keepdims=False) for r in range(dp)]
        )

    gains = jnp.concatenate([gain_one, gain_two])
    gain_rows = -(-gains.size // rows)
    gains = jnp.pad(gains, (0, gain_rows * rows - gains.size)).reshape(gain_rows, rows)
    pad_rows = -(q_cols + 2 * kv_cols + gain_rows) % 16
    qkv_block = jnp.concatenate(
        [query_weight.T, key_weight.T, value_weight.T, gains, jnp.zeros((pad_rows, rows), b16)]
    )
    qkv_all = gather(qkv_block, y_last)
    out_all = gather(output_weight.T, x_last)
    gu_all = gather(jnp.concatenate([gate_weight, up_weight], axis=1), x_last)
    down_all = gather(down_weight.T, y_last)

    first_gain = q_cols + 2 * kv_cols
    gain_all = qkv_all[0][:, first_gain : first_gain + gain_rows].reshape(ctx, -1)
    gain_part = gain_one.shape[0]
    gain_a = gain_all[:, :gain_part].reshape(1, width).astype(f32)
    gain_b = gain_all[:, gain_part : 2 * gain_part].reshape(1, width).astype(f32)
    qkv_all = [a.reshape(-1, rows) for a in qkv_all]
    out_all = [a.reshape(-1, rows) for a in out_all]
    down_all = [a.reshape(-1, down_rows) for a in down_all]

    cot = cotangent.reshape(total, width)
    cot_t = cot.T
    x_low = inputs.reshape(total, width)
    x = x_low.astype(f32)
    inv_one = lax.rsqrt(jnp.mean(x * x, axis=-1, keepdims=True) + epsilon)
    normed_one = (x * inv_one * gain_a).astype(b16)
    one_t = relative(normed_one.T.reshape(dp, rows, total))
    positions = (place * tokens + jnp.arange(tokens, dtype=jnp.int32)).astype(f32)
    positions = jnp.tile(positions, sequences)
    frequency = jnp.exp(jnp.arange(HALF, dtype=f32) * (-2.0 * math.log(rope_base) / HEAD_DIM))
    angles = frequency[:, None] * positions[None, :]
    cosine, sine = jnp.cos(angles), jnp.sin(angles)
    score_scale = HEAD_DIM ** (-0.5)
    seg_row = jnp.pad(segment_ids.reshape(1, total).astype(b16), ((0, 15), (0, 0)))
    block_rows = qkv_all[0].shape[0]
    q_rot, own = in_vmem(
        functools.partial(project_kernel, dp, q_cols, kv_cols, ctx, score_scale),
        "project",
        [shape_of((width, total), b16), shape_of((2 * kv_width + 16, total), b16)],
        [pltpu.VMEM((block_rows, total), f32), pltpu.VMEM((width + 2 * kv_width, total), f32)],
        one_t,
        *qkv_all,
        seg_row,
        cosine,
        sine,
    )

    steps = ctx // 4
    inner = bit("ctx", 1)
    straight = [own]
    for _ in range(steps):
        straight.append(shift_outer(straight[-1], 1))
    crossed = [
        swap(jnp.where(inner == 0, straight[k], straight[k + 1]), "ctx", 1) for k in range(steps)
    ]
    pieces = []
    for k in range(steps):
        pieces += [straight[k], crossed[k]]
    pieces.append(straight[steps])

    att, lse = attend(place_arg, q_rot, pieces, sequences, tokens)
    att_3 = att.reshape(dp, rows, total)

    mid, inv_two, normed_two = in_vmem(
        functools.partial(mix_kernel, dp),
        "mix",
        [shape_of((total, width), f32), shape_of((total, 1), f32), shape_of((total, width), b16)],
        [],
        me_arg,
        att_3,
        x_low,
        gain_b,
        *out_all,
        scalars=1,
    )
    two_t = relative(normed_two.T.reshape(dp, rows, total))
    two = jnp.transpose(two_t, (0, 2, 1))
    output, d_two, *grads = ffn(me_arg, two, two_t, cot, cot_t, mid, gu_all, down_all)
    g_gu = scatter(grads[:dp], x_last[::-1])
    g_down = scatter([g.reshape(ctx, out_cols, down_rows) for g in grads[dp:]], y_last[::-1])
    d_normed_two = jnp.transpose(relative(d_two), (1, 0, 2)).reshape(total, width)
    g_gain_two = jnp.sum(d_normed_two * mid * inv_two, axis=0)
    scaled_two = gain_b * d_normed_two
    d_mid = (
        cot.astype(f32)
        + inv_two * scaled_two
        - mid * inv_two**3 * jnp.mean(scaled_two * mid, axis=-1, keepdims=True)
    )
    d_att, *g_out = in_vmem(
        functools.partial(mix_back_kernel, dp),
        "mix_back",
        [shape_of(att_3.shape, b16)] + [shape_of((width, rows), b16)] * dp,
        [],
        me_arg,
        att_3,
        d_mid,
        *out_all,
        scalars=1,
    )
    g_out = scatter([g.reshape(ctx, out_cols, rows) for g in g_out], x_last[::-1])
    d_att = d_att.reshape(width, total)
    dq_rot, *parts = attend_back(place_arg, q_rot, d_att, lse, pieces, sequences, tokens)

    returned = [swap(parts[2 * k + 1], "ctx", 1).astype(f32) for k in range(steps)]
    here = []
    for k in range(steps + 1):
        value = parts[2 * k].astype(f32)
        if k < steps:
            value = value + jnp.where(inner == 0, returned[k], 0.0)
        if k > 0:
            value = value + jnp.where(inner == 1, returned[k - 1], 0.0)
        here.append(value)
    carried = here[steps]
    for k in range(steps, 0, -1):
        carried = here[k - 1] + shift_outer(carried.astype(b16), -1).astype(f32)

    d_one_t, *g_qkv = in_vmem(
        functools.partial(project_back_kernel, dp, q_cols, kv_cols, ctx, score_scale),
        "project_back",
        [shape_of((dp, rows, total), f32)] + [shape_of((block_rows, rows), b16)] * dp,
        [
            pltpu.VMEM((width + 2 * kv_width, total), f32),
            pltpu.VMEM((block_rows, total), b16),
        ],
        dq_rot,
        carried,
        cosine,
        sine,
        one_t,
        *qkv_all,
    )
    g_qkv = scatter([g.reshape(ctx, -1, rows) for g in g_qkv], y_last[::-1])
    d_normed_one = relative(d_one_t).reshape(width, total).T
    g_gain_one = jnp.sum(d_normed_one * x * inv_one, axis=0)
    scaled_one = gain_a * d_normed_one
    input_grad = (
        d_mid
        + inv_one * scaled_one
        - x * inv_one**3 * jnp.mean(scaled_one * x, axis=-1, keepdims=True)
    ).astype(b16)
    g_gains = sum_everywhere(jnp.stack([g_gain_one, g_gain_two]), dp_bits + ctx_bits)
    g_gains = lax.dynamic_slice_in_dim(g_gains, place * gain_part, gain_part, 1)
    return (
        output.reshape(sequences, tokens, width),
        input_grad.reshape(sequences, tokens, width),
        g_gains[0],
        g_qkv[:q_cols].T,
        g_qkv[q_cols : q_cols + kv_cols].T,
        g_qkv[q_cols + kv_cols : first_gain].T,
        g_out.T,
        g_gains[1],
        g_gu[:, :ff_cols],
        g_gu[:, ff_cols:],
        g_down.T,
    )


def solution(mesh):
    act = P("dp", "ctx", None)
    weight = P("dp", "ctx")
    gain = P("ctx")
    return jax.shard_map(
        per_device,
        mesh=mesh,
        in_specs=(
            act, gain, weight, weight, weight, weight, gain, weight, weight, weight, P("dp", "ctx"), act,
        ),
        out_specs=(
            act, act, gain, weight, weight, weight, weight, gain, weight, weight, weight,
        ),
        check_vma=False,
    )
```

```python
import functools
import math

import jax
import jax.numpy as jnp
from jax import lax
from jax.experimental import pallas as pl
from jax.experimental.pallas import tpu as pltpu
from jax.sharding import PartitionSpec as P

QUERY_HEADS = 15
KEY_VALUE_HEADS = 5
HEAD_DIM = 64
GROUP = QUERY_HEADS // KEY_VALUE_HEADS
HALF = HEAD_DIM // 2

epsilon = 1e-05
rope_base = 10000.0
masked = -1e30
f32 = jnp.float32
b16 = jnp.bfloat16


def bits_of(axis, size):
    masks = []
    mask = size // 2
    while mask:
        masks.append((axis, mask))
        mask //= 2
    return masks


def swap(values, axis, mask):
    size = lax.axis_size(axis)
    return lax.ppermute(values, axis, [(i, i ^ mask) for i in range(size)])


def bit(axis, mask):
    return (lax.axis_index(axis) // mask) % 2


def after(values, *others):
    return lax.optimization_barrier((values, *others))[0]


def higher(order, mask):
    return 2 ** sum(1 for axis, m in order if axis == "ctx" and m > mask)


class Gather:
    def __init__(self, block, order):
        self.bufs = {0: block[None]}
        self.order = order
        self.done = 0

    def step(self, *others):
        axis, mask = self.order[self.done]
        sent = {r: after(b, *others) if others else b for r, b in self.bufs.items()}
        got = {r: swap(b, axis, mask) for r, b in sent.items()}
        if axis == "dp":
            self.bufs = {**self.bufs, **{r ^ mask: b for r, b in got.items()}}
        else:
            upper = bit(axis, mask) == 1
            pre = higher(self.order[: self.done], mask)
            for r, theirs in got.items():
                mine = self.bufs[r]
                shape = (pre, 1, mine.shape[0] // pre) + mine.shape[1:]
                mine, theirs = mine.reshape(shape), theirs.reshape(shape)
                both = jnp.concatenate(
                    [jnp.where(upper, theirs, mine), jnp.where(upper, mine, theirs)], axis=1
                )
                self.bufs[r] = both.reshape((-1,) + shape[3:])
        self.done += 1
        return list(got.values())

    def result(self):
        return [self.bufs[r] for r in sorted(self.bufs)]


class Scatter:
    def __init__(self, bufs, order):
        self.bufs = dict(enumerate(bufs))
        self.order = order
        self.done = 0

    def step(self, *others, pieces=1, hold=()):
        axis, mask = self.order[self.done]
        rest = self.order[self.done + 1 :]
        if axis == "dp":
            keep = {r: b for r, b in self.bufs.items() if not r & mask}
            send = {r: self.bufs[r ^ mask] for r in keep}
        else:
            own = bit(axis, mask)
            pre = higher(rest, mask)
            keep, send = {}, {}
            for r, b in self.bufs.items():
                parts = b.reshape((pre, 2, b.shape[0] // (2 * pre)) + b.shape[1:])
                send[r], keep[r] = (
                    lax.dynamic_index_in_dim(parts, i, 1, keepdims=False).reshape(
                        (-1,) + b.shape[1:]
                    )
                    for i in (1 - own, own)
                )
        got = {}
        first = []
        for r, b in send.items():
            b = after(b, *others) if others else b
            if pieces == 1:
                got[r] = swap(b, axis, mask)
                first.append(got[r])
                continue
            half = b.shape[0] // 2
            lower = swap(b[:half], axis, mask)
            upper = swap(after(b[half:], lower), axis, mask)
            got[r] = jnp.concatenate([lower, upper])
            first.append(lower)
        self.bufs = {}
        for r in keep:
            other = after(got[r], *hold) if hold else got[r]
            total = keep[r].astype(f32) + other.astype(f32)
            self.bufs[r] = total.astype(b16) if rest else total
        self.done += 1
        return first

    def finish(self):
        while self.done < len(self.order):
            self.step()
        return self.bufs[0][0]


def shift_outer(values, by):
    size = lax.axis_size("ctx")
    return lax.ppermute(
        values, "ctx", [(i, i + 2 * by) for i in range(size) if 0 <= i + 2 * by < size]
    )


def dot(a, b, dims):
    return lax.dot_general(a, b, (dims, ((), ())), preferred_element_type=f32)


def fill_bias(blocks, tokens, place, seg_refs, bias):
    queries = jnp.broadcast_to(seg_refs[0][0:1, :].astype(f32), (tokens, tokens))
    for j in range(blocks):
        keys = jnp.broadcast_to(seg_refs[j][0:1, :].astype(f32), (tokens, tokens)).T
        allowed = (keys == queries) & (place >= j)
        if j == 0:
            key_row = lax.broadcasted_iota(jnp.int32, (tokens, tokens), 0)
            query_col = lax.broadcasted_iota(jnp.int32, (tokens, tokens), 1)
            allowed = allowed & (key_row <= query_col)
        bias[j * tokens : (j + 1) * tokens, :] = jnp.where(allowed, 0.0, masked)


def heads_side(ref):
    return jnp.concatenate(
        [ref[h * HEAD_DIM : (h + 1) * HEAD_DIM, :] for h in range(GROUP)], axis=1
    )


def forward_kernel(blocks, tokens, place_ref, *refs):
    q_ref = refs[0]
    k_refs = refs[1 : 1 + blocks]
    v_refs = refs[1 + blocks : 1 + 2 * blocks]
    seg_refs = refs[1 + 2 * blocks : 1 + 3 * blocks]
    att_ref, lse_ref, bias = refs[1 + 3 * blocks :]

    @pl.when(pl.program_id(1) == 0)
    def _():
        fill_bias(blocks, tokens, place_ref[0], seg_refs, bias)

    keys = jnp.concatenate([r[...] for r in k_refs], axis=1)
    values = jnp.concatenate([r[...] for r in v_refs], axis=1)
    scores = dot(keys, heads_side(q_ref), ((0,), (0,)))
    for h in range(GROUP):
        own = scores[:, h * tokens : (h + 1) * tokens] + bias[...]
        top = jnp.max(own, axis=0, keepdims=True)
        probs = jnp.exp(own - top)
        total = jnp.sum(probs, axis=0, keepdims=True)
        out = dot(values, probs.astype(b16), ((1,), (0,)))
        att_ref[h * HEAD_DIM : (h + 1) * HEAD_DIM, :] = (out / total).astype(b16)
        lse_ref[0, h : h + 1, :] = top + jnp.log(total)


def backward_kernel(blocks, tokens, place_ref, *refs):
    q_ref, datt_ref, lse_ref = refs[:3]
    k_refs = refs[3 : 3 + blocks]
    v_refs = refs[3 + blocks : 3 + 2 * blocks]
    seg_refs = refs[3 + 2 * blocks : 3 + 3 * blocks]
    dq_ref = refs[3 + 3 * blocks]
    dkv_refs = refs[4 + 3 * blocks : 4 + 4 * blocks]
    bias, p_scr, ds_scr = refs[4 + 4 * blocks :]

    @pl.when(pl.program_id(1) == 0)
    def _():
        fill_bias(blocks, tokens, place_ref[0], seg_refs, bias)

    keys = jnp.concatenate([r[...] for r in k_refs], axis=1)
    values = jnp.concatenate([r[...] for r in v_refs], axis=1)
    queries = heads_side(q_ref)
    grads = heads_side(datt_ref)
    scores = dot(keys, queries, ((0,), (0,)))
    d_probs = dot(values, grads, ((0,), (0,)))
    for h in range(GROUP):
        lanes = slice(h * tokens, (h + 1) * tokens)
        probs = jnp.exp(scores[:, lanes] + bias[...] - lse_ref[0, h : h + 1, :])
        weighted = probs * d_probs[:, lanes]
        delta = jnp.sum(weighted, axis=0, keepdims=True)
        p_scr[:, lanes] = probs.astype(b16)
        ds_scr[:, lanes] = (weighted - probs * delta).astype(b16)
    d_scores = ds_scr[...]
    dq = dot(keys, d_scores, ((1,), (0,)))
    for h in range(GROUP):
        dq_ref[h * HEAD_DIM : (h + 1) * HEAD_DIM, :] = dq[:, h * tokens : (h + 1) * tokens]
    dk = dot(queries, d_scores, ((1,), (1,)))
    dv = dot(grads, p_scr[...], ((1,), (1,)))
    for j in range(blocks):
        lanes = slice(j * tokens, (j + 1) * tokens)
        dkv_refs[j][0] = dk[:, lanes].astype(b16)
        dkv_refs[j][1] = dv[:, lanes].astype(b16)


def kv_specs(blocks, tokens):
    per_group = (HEAD_DIM, tokens)
    key = pl.BlockSpec(per_group, lambda s, g, _: (g, s))
    value = pl.BlockSpec(per_group, lambda s, g, _: (KEY_VALUE_HEADS + g, s))
    seg_row = 2 * KEY_VALUE_HEADS * HEAD_DIM // 16
    seg = pl.BlockSpec((16, tokens), lambda s, g, _: (seg_row, s))
    return [key] * blocks + [value] * blocks + [seg] * blocks


def attend(place, q_rot, pieces, sequences, tokens):
    blocks = len(pieces)
    heads = pl.BlockSpec((GROUP * HEAD_DIM, tokens), lambda s, g, _: (g, s))
    stat = pl.BlockSpec((1, 8, tokens), lambda s, g, _: (g, 0, s))
    wide = sequences * tokens
    return pl.pallas_call(
        functools.partial(forward_kernel, blocks, tokens),
        grid_spec=pltpu.PrefetchScalarGridSpec(
            num_scalar_prefetch=1,
            grid=(sequences, KEY_VALUE_HEADS),
            in_specs=[heads] + kv_specs(blocks, tokens),
            out_specs=[heads, stat],
            scratch_shapes=[pltpu.VMEM((blocks * tokens, tokens), f32)],
        ),
        out_shape=[
            jax.ShapeDtypeStruct((QUERY_HEADS * HEAD_DIM, wide), b16),
            jax.ShapeDtypeStruct((KEY_VALUE_HEADS, 8, wide), f32),
        ],
        compiler_params=pltpu.CompilerParams(vmem_limit_bytes=40 << 20),
        cost_estimate=pl.CostEstimate(flops=1, bytes_accessed=1, transcendentals=0),
        name="attend",
    )(place, q_rot, *pieces, *pieces, *pieces)


def attend_back(place, q_rot, datt, lse, pieces, sequences, tokens):
    blocks = len(pieces)
    heads = pl.BlockSpec((GROUP * HEAD_DIM, tokens), lambda s, g, _: (g, s))
    stat = pl.BlockSpec((1, 8, tokens), lambda s, g, _: (g, 0, s))
    pair = pl.BlockSpec((2, HEAD_DIM, tokens), lambda s, g, _: (0, g, s))
    wide = sequences * tokens
    return pl.pallas_call(
        functools.partial(backward_kernel, blocks, tokens),
        grid_spec=pltpu.PrefetchScalarGridSpec(
            num_scalar_prefetch=1,
            grid=(sequences, KEY_VALUE_HEADS),
            in_specs=[heads, heads, stat] + kv_specs(blocks, tokens),
            out_specs=[heads] + [pair] * blocks,
            scratch_shapes=[
                pltpu.VMEM((blocks * tokens, tokens), f32),
                pltpu.VMEM((blocks * tokens, GROUP * tokens), b16),
                pltpu.VMEM((blocks * tokens, GROUP * tokens), b16),
            ],
        ),
        out_shape=[jax.ShapeDtypeStruct((QUERY_HEADS * HEAD_DIM, wide), f32)]
        + [jax.ShapeDtypeStruct((2, KEY_VALUE_HEADS * HEAD_DIM, wide), b16)] * blocks,
        compiler_params=pltpu.CompilerParams(vmem_limit_bytes=48 << 20),
        cost_estimate=pl.CostEstimate(flops=1, bytes_accessed=1, transcendentals=0),
        name="attend_back",
    )(place, q_rot, datt, lse, *pieces, *pieces, *pieces)


def turned(low, high, cosine, sine, sign):
    return low * cosine - sign * high * sine, high * cosine + sign * low * sine


def turn_rows(source, target, heads, cosine, sine, sign, scale):
    for h in range(heads):
        at = h * HEAD_DIM
        low, high = source[at : at + HALF], source[at + HALF : at + HEAD_DIM]
        pair = turned(low, high, cosine, sine, sign)
        for i, half in enumerate(pair):
            rows = slice(at + i * HALF, at + (i + 1) * HALF)
            target[rows] = (half * scale).astype(target.dtype)


def project_kv_kernel(parts, kv_cols, ctx, *refs):
    x_ref, inv_ref, gain_ref = refs[:3]
    w_refs = refs[3 : 3 + parts]
    seg_ref, cos_ref, sin_ref, normed_ref, own_ref, blocks, flat = refs[3 + parts :]
    for r in range(parts):
        normed = (x_ref[r].astype(f32) * inv_ref[...] * gain_ref[r]).astype(b16)
        normed_ref[r] = normed
        part = dot(w_refs[r][...], normed, ((1,), (0,)))
        if r == 0:
            blocks[...] = part
        else:
            blocks[...] += part
    rows = blocks.shape[0] // ctx
    kv_width = KEY_VALUE_HEADS * HEAD_DIM
    for c in range(ctx):
        base, at = c * rows, c * kv_cols
        flat[at : at + kv_cols] = blocks[base : base + kv_cols]
        at += kv_width
        flat[at : at + kv_cols] = blocks[base + kv_cols : base + 2 * kv_cols]
    turn_rows(flat, own_ref, KEY_VALUE_HEADS, cos_ref[...], sin_ref[...], 1.0, 1.0)
    own_ref[kv_width : 2 * kv_width] = flat[kv_width : 2 * kv_width].astype(b16)
    own_ref[2 * kv_width : 2 * kv_width + 16] = seg_ref[...]


def project_q_kernel(parts, scale, normed_ref, cos_ref, sin_ref, *refs):
    w_refs = refs[:parts]
    q_ref, flat = refs[parts:]
    acc = dot(w_refs[0][...], normed_ref[0], ((1,), (0,)))
    for r in range(1, parts):
        acc = acc + dot(w_refs[r][...], normed_ref[r], ((1,), (0,)))
    flat[...] = acc
    turn_rows(flat, q_ref, QUERY_HEADS, cos_ref[...], sin_ref[...], 1.0, scale)


def project_q_back_kernel(parts, scale, dq_ref, normed_ref, cos_ref, sin_ref, *refs):
    w_refs = refs[:parts]
    dn_ref = refs[parts]
    g_refs = refs[1 + parts : 1 + 2 * parts]
    flat = refs[1 + 2 * parts]
    turn_rows(dq_ref, flat, QUERY_HEADS, cos_ref[...], sin_ref[...], -1.0, scale)
    for r in range(parts):
        g_refs[r][...] = dot(flat[...], normed_ref[r], ((1,), (1,))).astype(b16)
    for r in range(parts):
        dn_ref[r] = dot(w_refs[r][...], flat[...], ((0,), (0,)))


def project_kv_back_kernel(parts, kv_cols, ctx, me_ref, *refs):
    dkv_ref, cos_ref, sin_ref, normed_ref, dn_q_ref, x_ref, inv_ref, gain_ref, d_mid_ref = refs[:9]
    w_refs = refs[9 : 9 + parts]
    out_ref, g_gain_ref = refs[9 + parts : 11 + parts]
    g_refs = refs[11 + parts : 11 + 2 * parts]
    flat, blocks, d_x = refs[11 + 2 * parts :]
    kv_width = KEY_VALUE_HEADS * HEAD_DIM
    turn_rows(dkv_ref.at[0], flat, KEY_VALUE_HEADS, cos_ref[...], sin_ref[...], -1.0, 1.0)
    rows = blocks.shape[0] // ctx
    for c in range(ctx):
        base, at = c * rows, c * kv_cols
        blocks[base : base + kv_cols] = flat[at : at + kv_cols]
        blocks[base + kv_cols : base + 2 * kv_cols] = dkv_ref[1, at : at + kv_cols]
        blocks[base + 2 * kv_cols : base + rows] = jnp.zeros(
            (rows - 2 * kv_cols, blocks.shape[1]), f32
        )
    low = blocks[...].astype(b16)
    for r in range(parts):
        g_refs[r][...] = dot(low, normed_ref[r], ((1,), (1,))).astype(b16)
    inv = inv_ref[...]
    mean = jnp.zeros_like(inv)
    for r in range(parts):
        d_normed = dn_q_ref[r] + dot(w_refs[r][...], low, ((0,), (0,)))
        x = x_ref[r].astype(f32)
        g_gain_ref[r] = jnp.sum(d_normed * (x * inv), axis=1, keepdims=True)
        scaled = d_normed * gain_ref[r]
        d_x[r] = scaled
        mean = mean + jnp.sum(scaled * x, axis=0, keepdims=True)
    mean = mean / (parts * x_ref.shape[1]) * (inv * inv * inv)
    pieces = []
    for d in range(parts):
        r = me_ref[0] ^ d
        total = d_mid_ref[d] + inv * d_x[r] - x_ref[r].astype(f32) * mean
        pieces.append(total.T)
    out_ref[...] = jnp.concatenate(pieces, axis=1).astype(b16)


def mix_kernel(parts, me_ref, att_ref, x_ref, gain_ref, *refs):
    w_refs = refs[:parts]
    mid_ref, inv_ref, normed_ref, normed_t_ref = refs[parts:]
    mid = x_ref[...].astype(f32)
    for r in range(parts):
        mid = mid + dot(att_ref[me_ref[0] ^ r], w_refs[r][...], ((0,), (1,)))
    mid_ref[...] = mid
    inv = lax.rsqrt(jnp.mean(mid * mid, axis=-1, keepdims=True) + epsilon)
    inv_ref[...] = inv
    normed = mid * inv * gain_ref[...]
    rows = normed_ref.shape[2]
    for d in range(parts):
        part = normed[:, d * rows : (d + 1) * rows]
        normed_ref[me_ref[0] ^ d] = part.astype(b16)
        normed_t_ref[me_ref[0] ^ d] = part.T.astype(b16)


def mix_back_kernel(parts, me_ref, att_ref, cot_ref, mid_ref, inv_ref, gain_ref, dn_ref, *refs):
    w_refs = refs[:parts]
    datt_ref, d_mid_ref, g_gain_ref = refs[parts : 3 + parts]
    g_refs = refs[3 + parts : 3 + 2 * parts]
    flipped = refs[3 + 2 * parts]
    rows = dn_ref.shape[2]
    inv = inv_ref[...]
    mean = jnp.zeros_like(inv)
    for d in range(parts):
        lanes = slice(d * rows, (d + 1) * rows)
        d_normed = dn_ref[me_ref[0] ^ d]
        mid = mid_ref[:, lanes]
        g_gain_ref[d] = jnp.sum(d_normed * (mid * inv), axis=0, keepdims=True)
        mean = mean + jnp.sum(d_normed * gain_ref[:, lanes] * mid, axis=-1, keepdims=True)
    mean = mean / (parts * rows) * (inv * inv * inv)
    for d in range(parts):
        lanes = slice(d * rows, (d + 1) * rows)
        scaled = dn_ref[me_ref[0] ^ d] * gain_ref[:, lanes]
        d_mid = cot_ref[:, lanes].astype(f32) + inv * scaled - mid_ref[:, lanes] * mean
        d_mid = d_mid.T
        d_mid_ref[d] = d_mid
        flipped[lanes] = d_mid.astype(b16)
    for r in range(parts):
        at = me_ref[0] ^ r
        g_refs[r][...] = dot(flipped[...], att_ref[at], ((1,), (1,))).astype(b16)
        datt_ref[at] = dot(w_refs[r][...], flipped[...], ((0,), (0,))).astype(b16)


def ffn_kernel(parts, per, me_ref, n_ref, nt_ref, cot_ref, mid_ref, *refs):
    f_refs = [refs[:parts], refs[parts : 2 * parts]]
    d_refs = refs[2 * parts : 3 * parts]
    out_ref, dn_ref = refs[3 * parts : 3 * parts + 2]
    rest = refs[3 * parts + 2 :]
    gf_refs = [rest[:parts], rest[parts : 2 * parts]]
    gd_refs = rest[2 * parts : 3 * parts]
    acc, down, g_down, hidden, cot_t = rest[3 * parts :]
    step = pl.program_id(0)
    for r in range(parts):

        @pl.when(step == r)
        def _(r=r):
            down[...] = d_refs[r][...]

    @pl.when(step == 0)
    def _():
        acc[...] = jnp.zeros_like(acc)
        cot_t[...] = cot_ref[...].T
        dn_ref[...] = jnp.zeros_like(dn_ref)

    cut = f_refs[0][0].shape[2]
    ff = (cut + f_refs[1][0].shape[2]) // 2
    d_hidden = dot(cot_ref[...], down[...], ((1,), (0,)))
    for i in range(per):
        both = []
        for side in f_refs:
            part = dot(n_ref[0], side[0][i], ((1,), (0,)))
            for r in range(1, parts):
                part = part + dot(n_ref[r], side[r][i], ((1,), (0,)))
            both.append(part)
        both = jnp.concatenate(both, axis=1)
        gate, up = both[:, :ff], both[:, ff:]
        grad = d_hidden[:, i * ff : (i + 1) * ff]
        sigma = jax.nn.sigmoid(gate)
        silu = gate * sigma
        hidden[:, i * ff : (i + 1) * ff] = (silu * up).astype(b16)
        d_gate = grad * up * (sigma * (1.0 + gate * (1.0 - sigma)))
        d_both = jnp.concatenate([d_gate, grad * silu], axis=1).astype(b16)
        sides = (d_both[:, :cut], d_both[:, cut:])
        for r in range(parts):
            for side in range(2):
                grad = dot(nt_ref[r], sides[side], ((1,), (0,)))
                gf_refs[side][r][i] = grad.astype(b16)
            dn_ref[r] += dot(sides[0], f_refs[0][r][i], ((1,), (1,))) + dot(
                sides[1], f_refs[1][r][i], ((1,), (1,))
            )
    acc[...] += dot(hidden[...], down[...], ((1,), (1,)))
    g_down[...] = dot(cot_t[...], hidden[...], ((1,), (0,))).astype(b16)
    for r in range(parts):

        @pl.when(step == r)
        def _(r=r):
            gd_refs[r][...] = g_down[...]

    @pl.when(step == parts - 1)
    def _():
        out_ref[...] = (mid_ref[...] + acc[...]).astype(b16)


def ffn(me, n_rel, nt_rel, cot, mid, f_one, f_two, d_list):
    parts = len(f_one)
    ctx, rows, cut = f_one[0].shape
    wide = cut + f_two[0].shape[2]
    per = ctx // parts
    tokens, width = mid.shape
    down_shape = d_list[0].shape

    def whole(a):
        return pl.BlockSpec(a.shape, lambda i, me: (0,) * a.ndim, pipeline_mode=pl.Buffered(1))

    f_specs = [
        pl.BlockSpec((per, rows, n), lambda i, me: (me[0] ^ i, 0, 0))
        for n in [cut] * parts + [wide - cut] * parts
    ]
    out_shape = [
        jax.ShapeDtypeStruct((tokens, width), b16),
        jax.ShapeDtypeStruct((parts, tokens, rows), f32),
    ]
    out_shape += [jax.ShapeDtypeStruct(f.shape, b16) for f in f_one + f_two]
    out_shape += [jax.ShapeDtypeStruct(down_shape, b16)] * parts
    return pl.pallas_call(
        functools.partial(ffn_kernel, parts, per),
        grid_spec=pltpu.PrefetchScalarGridSpec(
            num_scalar_prefetch=1,
            grid=(parts,),
            in_specs=[whole(a) for a in (n_rel, nt_rel, cot, mid)]
            + f_specs
            + [whole(a) for a in d_list],
            out_specs=[whole(a) for a in out_shape[:2]]
            + f_specs
            + [whole(a) for a in d_list],
            scratch_shapes=[
                pltpu.VMEM((tokens, width), f32),
                pltpu.VMEM(down_shape, b16),
                pltpu.VMEM(down_shape, b16),
                pltpu.VMEM((tokens, per * wide // 2), b16),
                pltpu.VMEM((width, tokens), b16),
            ],
        ),
        out_shape=out_shape,
        compiler_params=pltpu.CompilerParams(vmem_limit_bytes=58 << 20),
        cost_estimate=pl.CostEstimate(flops=1, bytes_accessed=1, transcendentals=0),
        name="ffn",
    )(me, n_rel, nt_rel, cot, mid, *f_one, *f_two, *d_list)


def in_vmem(kernel, name, out_shape, scratch, *args, scalars=0):
    vmem = pl.BlockSpec(memory_space=pltpu.VMEM)
    smem = pl.BlockSpec(memory_space=pltpu.SMEM)
    return pl.pallas_call(
        kernel,
        in_specs=[smem] * scalars + [vmem] * (len(args) - scalars),
        out_specs=[vmem] * len(out_shape),
        out_shape=out_shape,
        scratch_shapes=scratch,
        compiler_params=pltpu.CompilerParams(vmem_limit_bytes=48 << 20),
        cost_estimate=pl.CostEstimate(flops=1, bytes_accessed=1, transcendentals=0),
        name=name,
    )(*args)


def per_device(
    inputs,
    gain_one,
    query_weight,
    key_weight,
    value_weight,
    output_weight,
    gain_two,
    gate_weight,
    up_weight,
    down_weight,
    segment_ids,
    cotangent,
):
    dp, ctx = lax.axis_size("dp"), lax.axis_size("ctx")
    sequences, tokens, width = inputs.shape
    total = sequences * tokens
    rows = query_weight.shape[0]
    q_cols, kv_cols = query_weight.shape[1], key_weight.shape[1]
    ff_cols = gate_weight.shape[1]
    down_rows, out_cols = down_weight.shape
    kv_width = KEY_VALUE_HEADS * HEAD_DIM
    shape_of = jax.ShapeDtypeStruct

    dp_bits, ctx_bits = bits_of("dp", dp), bits_of("ctx", ctx)
    x_last = ctx_bits + dp_bits
    y_last = ctx_bits[:-1] + dp_bits[:-1] + ctx_bits[-1:] + dp_bits[-1:]
    z_last = ctx_bits[:-2] + ctx_bits[-1:] + dp_bits[:-1] + ctx_bits[-2:-1] + dp_bits[-1:]

    place = lax.axis_index("ctx")
    me = lax.axis_index("dp")
    me_arg = me.reshape(1).astype(jnp.int32)
    place_arg = place.reshape(1).astype(jnp.int32)

    def relative(stacked):
        return jnp.stack(
            [lax.dynamic_index_in_dim(stacked, me ^ r, 0, keepdims=False) for r in range(dp)]
        )

    gains = jnp.concatenate([gain_one, gain_two])
    gain_rows = -(-gains.size // rows)
    gains = jnp.pad(gains, (0, gain_rows * rows - gains.size)).reshape(gain_rows, rows)
    pad_rows = -(2 * kv_cols + gain_rows) % 8
    kv_block = jnp.concatenate(
        [key_weight.T, value_weight.T, gains, jnp.zeros((pad_rows, rows), b16)]
    )
    kv_gather = Gather(kv_block, y_last)
    qo_gather = Gather(jnp.concatenate([query_weight.T, output_weight.T]), x_last)
    gate_up = jnp.concatenate([gate_weight, up_weight], axis=1)
    cut = max(2 * ff_cols * 3 // 5 // 128, 1) * 128
    one_gather = Gather(gate_up[:, :cut], x_last)
    two_gather = Gather(gate_up[:, cut:], y_last)
    down_gather = Gather(down_weight.T, z_last)
    outer = len(ctx_bits) - 1
    token = kv_gather.step()
    one_gather.step(*token)
    two_gather.step(*token)
    token = kv_gather.step()
    down_gather.step(*token)
    qo_gather.step(*token)
    while kv_gather.done < len(x_last) - 1:
        token = kv_gather.step()
    for _ in range(outer - 1):
        two_gather.step(*token)
        down_gather.step(*token)
        one_gather.step(*token)
        qo_gather.step(*token)
    kv_gather.step()
    kv_all = kv_gather.result()

    first_gain = 2 * kv_cols
    gain_all = kv_all[0][:, first_gain : first_gain + gain_rows].reshape(ctx, -1)
    gain_part = gain_one.shape[0]
    gain_a = relative(gain_all[:, :gain_part].reshape(dp, rows, 1).astype(f32))
    gain_b = gain_all[:, gain_part : 2 * gain_part].reshape(1, width).astype(f32)
    kv_all = [a.reshape(-1, rows) for a in kv_all]

    cot = cotangent.reshape(total, width)
    x_low = inputs.reshape(total, width)
    x = x_low.astype(f32)
    inv_one = lax.rsqrt(jnp.mean(x * x, axis=-1) + epsilon).reshape(1, total)
    x_t = relative(x_low.T.reshape(dp, rows, total))
    positions = (place * tokens + jnp.arange(tokens, dtype=jnp.int32)).astype(f32)
    positions = jnp.tile(positions, sequences)
    frequency = jnp.exp(jnp.arange(HALF, dtype=f32) * (-2.0 * math.log(rope_base) / HEAD_DIM))
    angles = frequency[:, None] * positions[None, :]
    cosine, sine = jnp.cos(angles), jnp.sin(angles)
    score_scale = HEAD_DIM ** (-0.5)
    seg_row = jnp.pad(segment_ids.reshape(1, total).astype(b16), ((0, 15), (0, 0)))
    block_rows = kv_all[0].shape[0]
    one_t, own = in_vmem(
        functools.partial(project_kv_kernel, dp, kv_cols, ctx),
        "project_kv",
        [shape_of((dp, rows, total), b16), shape_of((2 * kv_width + 16, total), b16)],
        [pltpu.VMEM((block_rows, total), f32), pltpu.VMEM((2 * kv_width, total), f32)],
        x_t,
        inv_one,
        gain_a,
        *kv_all,
        seg_row,
        cosine,
        sine,
    )

    steps = ctx // 4
    inner = bit("ctx", 1)
    straight = [own]
    for _ in range(steps):
        straight.append(shift_outer(straight[-1], 1))
    crossed = [
        swap(jnp.where(inner == 0, straight[k], straight[k + 1]), "ctx", 1) for k in range(steps)
    ]
    while two_gather.done < len(x_last) - 2:
        spread = two_gather.step()
    while down_gather.done < len(x_last) - 2:
        spread += down_gather.step()
    while one_gather.done < outer + 1:
        one_gather.step()
    while qo_gather.done < outer + 1:
        qo_gather.step()
    ahead = qo_gather.step(*spread)
    while qo_gather.done < len(x_last):
        qo_gather.step()
    q_all = [a[:, :q_cols].reshape(-1, rows) for a in qo_gather.result()]
    out_all = [a[:, q_cols:].reshape(-1, rows) for a in qo_gather.result()]
    (q_rot,) = in_vmem(
        functools.partial(project_q_kernel, dp, score_scale),
        "project_q",
        [shape_of((width, total), b16)],
        [pltpu.VMEM((width, total), f32)],
        after(one_t, straight[1]),
        cosine,
        sine,
        *q_all,
    )
    one_gather.step(*ahead, straight[1])
    down_gather.step(straight[steps])
    two_gather.step(*crossed)
    pieces = []
    for k in range(steps):
        pieces += [straight[k], crossed[k]]
    pieces.append(straight[steps])

    att, lse = attend(place_arg, q_rot, pieces, sequences, tokens)
    for g in (one_gather, two_gather, down_gather):
        while g.done < len(x_last):
            g.step(lse)
    down_all = [a.reshape(-1, down_rows) for a in down_gather.result()]
    att_3 = att.reshape(dp, rows, total)

    mid, inv_two, two, two_t = in_vmem(
        functools.partial(mix_kernel, dp),
        "mix",
        [
            shape_of((total, width), f32),
            shape_of((total, 1), f32),
            shape_of((dp, total, rows), b16),
            shape_of((dp, rows, total), b16),
        ],
        [],
        me_arg,
        att_3,
        x_low,
        gain_b,
        *out_all,
        scalars=1,
    )
    output, d_two, *grads = ffn(me_arg, two, two_t, cot, mid, one_gather.result(), two_gather.result(), down_all)
    g_one = Scatter(grads[:dp], x_last[::-1])
    g_two = Scatter(grads[dp : 2 * dp], y_last[::-1])
    g_down = Scatter([g.reshape(ctx, out_cols, down_rows) for g in grads[2 * dp :]], z_last[::-1])
    d_att, d_mid, g_gain_two, *g_out = in_vmem(
        functools.partial(mix_back_kernel, dp),
        "mix_back",
        [
            shape_of(att_3.shape, b16),
            shape_of((dp, rows, total), f32),
            shape_of((dp, 1, rows), f32),
        ]
        + [shape_of((width, rows), b16)] * dp,
        [pltpu.VMEM((width, total), b16)],
        me_arg,
        att_3,
        cot,
        mid,
        inv_two,
        gain_b,
        d_two,
        *out_all,
        scalars=1,
    )
    folded = g_one.step(hold=(d_att,))
    folded += [t for g in (g_two, g_down) for t in g.step(hold=(d_att, *folded[:1]))]
    d_att = after(d_att.reshape(width, total), *folded)
    under_x, under_y, under_z = g_one.step(), g_two.step(), g_down.step()
    dq_rot, *parts = attend_back(place_arg, q_rot, d_att, lse, pieces, sequences, tokens)
    dq_rot = after(dq_rot, *under_x, *under_y, *under_z)
    parts = [after(p, *under_y) for p in parts]
    dn_q, *g_q = in_vmem(
        functools.partial(project_q_back_kernel, dp, score_scale),
        "project_q_back",
        [shape_of((dp, rows, total), f32)] + [shape_of((width, rows), b16)] * dp,
        [pltpu.VMEM((width, total), b16)],
        dq_rot,
        one_t,
        cosine,
        sine,
        *q_all,
    )

    returned = [swap(parts[2 * k + 1], "ctx", 1).astype(f32) for k in range(steps)]
    here = []
    for k in range(steps + 1):
        value = parts[2 * k].astype(f32)
        if k < steps:
            value = value + jnp.where(inner == 0, returned[k], 0.0)
        if k > 0:
            value = value + jnp.where(inner == 1, returned[k - 1], 0.0)
        here.append(value)
    carried = here[steps]
    for k in range(steps, 0, -1):
        moved = shift_outer(carried.astype(b16), -1)
        if k == steps:
            first_moved = moved
        carried = here[k - 1] + moved.astype(f32)
    g_qo = [
        jnp.concatenate([q.reshape(ctx, q_cols, rows), o.reshape(ctx, out_cols, rows)], axis=1)
        for q, o in zip(g_q, g_out, strict=True)
    ]
    g_qo = Scatter(g_qo, x_last[::-1])
    g_qo.step(parts[0])
    beside = g_two.step() + g_down.step() + g_one.step(*returned)
    beside += g_qo.step(*beside[:2])
    for g in (g_two, g_down, g_one):
        g.step(first_moved)
    while g_one.done < len(x_last):
        for g in (g_two, g_down, g_one):
            g.step(carried)

    carried = after(carried, *beside)
    input_grad, g_gain_one, *g_kv = in_vmem(
        functools.partial(project_kv_back_kernel, dp, kv_cols, ctx),
        "project_kv_back",
        [shape_of((total, width), b16), shape_of((dp, rows, 1), f32)]
        + [shape_of((block_rows, rows), b16)] * dp,
        [
            pltpu.VMEM((kv_width, total), f32),
            pltpu.VMEM((block_rows, total), f32),
            pltpu.VMEM((dp, rows, total), f32),
        ],
        me_arg,
        carried,
        cosine,
        sine,
        one_t,
        dn_q,
        x_t,
        inv_one,
        gain_a,
        d_mid,
        *kv_all,
        scalars=1,
    )
    g_gains = jnp.concatenate(
        [relative(g_gain_one).reshape(ctx, gain_part), g_gain_two.reshape(ctx, gain_part)], axis=1
    ).astype(b16)
    g_gains = jnp.pad(g_gains, ((0, 0), (0, gain_rows * rows - 2 * gain_part)))
    g_gains = jnp.pad(g_gains.reshape(ctx, gain_rows, rows), ((0, 0), (0, pad_rows), (0, 0)))
    g_kv = [
        jnp.concatenate([g.reshape(ctx, -1, rows)[:, :first_gain], g_gains], axis=1) for g in g_kv
    ]
    g_kv = Scatter(g_kv, x_last[::-1])
    token = g_kv.step()
    early = g_qo.step()
    while g_kv.done < len(x_last):
        token = g_kv.step(*token)
        if g_qo.done < min(g_kv.done, len(x_last)):
            g_qo.step(*token)
    g_kv, g_qo, g_down = g_kv.finish(), g_qo.finish(), g_down.finish()
    g_gu = jnp.concatenate([g_one.finish(), g_two.finish()], axis=1)
    g_gains = g_kv[first_gain : first_gain + gain_rows].reshape(-1)
    return (
        output.reshape(sequences, tokens, width),
        input_grad.reshape(sequences, tokens, width),
        g_gains[:gain_part],
        g_qo[:q_cols].T,
        g_kv[:kv_cols].T,
        g_kv[kv_cols : 2 * kv_cols].T,
        g_qo[q_cols:].T,
        g_gains[gain_part : 2 * gain_part],
        g_gu[:, :ff_cols],
        g_gu[:, ff_cols:],
        g_down.T,
    )


def solution(mesh):
    act = P("dp", "ctx", None)
    weight = P("dp", "ctx")
    gain = P("ctx")
    return jax.shard_map(
        per_device,
        mesh=mesh,
        in_specs=(
            act, gain, weight, weight, weight, weight, gain, weight, weight, weight, P("dp", "ctx"), act,
        ),
        out_specs=(
            act, act, gain, weight, weight, weight, weight, gain, weight, weight, weight,
        ),
        check_vma=False,
    )
```

```python
import functools
import math

import jax
import jax.numpy as jnp
from jax import lax
from jax.experimental import pallas as pl
from jax.experimental.pallas import tpu as pltpu
from jax.sharding import PartitionSpec as P

QUERY_HEADS = 15
KEY_VALUE_HEADS = 5
HEAD_DIM = 64
GROUP = QUERY_HEADS // KEY_VALUE_HEADS
HALF = HEAD_DIM // 2

epsilon = 1e-05
rope_base = 10000.0
masked = -1e30
f32 = jnp.float32
b16 = jnp.bfloat16


def bits_of(axis, size):
    masks = []
    mask = size // 2
    while mask:
        masks.append((axis, mask))
        mask //= 2
    return masks


def swap(values, axis, mask):
    size = lax.axis_size(axis)
    return lax.ppermute(values, axis, [(i, i ^ mask) for i in range(size)])


def bit(axis, mask):
    return (lax.axis_index(axis) // mask) % 2


def after(values, *others):
    return lax.optimization_barrier((values, *others))[0]


def higher(order, mask):
    return 2 ** sum(1 for axis, m in order if axis == "ctx" and m > mask)


class Gather:
    def __init__(self, block, order):
        self.bufs = {0: block[None]}
        self.order = order
        self.done = 0

    def step(self, *others, hold=()):
        axis, mask = self.order[self.done]
        sent = {r: after(b, *others) if others else b for r, b in self.bufs.items()}
        got = {r: swap(b, axis, mask) for r, b in sent.items()}
        if hold:
            got = {r: after(b, *hold) for r, b in got.items()}
        if axis == "dp":
            self.bufs = {**self.bufs, **{r ^ mask: b for r, b in got.items()}}
        else:
            upper = bit(axis, mask) == 1
            pre = higher(self.order[: self.done], mask)
            for r, theirs in got.items():
                mine = self.bufs[r]
                shape = (pre, 1, mine.shape[0] // pre) + mine.shape[1:]
                mine, theirs = mine.reshape(shape), theirs.reshape(shape)
                both = jnp.concatenate(
                    [jnp.where(upper, theirs, mine), jnp.where(upper, mine, theirs)], axis=1
                )
                self.bufs[r] = both.reshape((-1,) + shape[3:])
        self.done += 1
        return list(got.values())

    def result(self):
        return [self.bufs[r] for r in sorted(self.bufs)]


class Scatter:
    def __init__(self, bufs, order):
        self.bufs = dict(enumerate(bufs))
        self.order = order
        self.done = 0

    def step(self, *others, pieces=1, hold=()):
        axis, mask = self.order[self.done]
        rest = self.order[self.done + 1 :]
        if axis == "dp":
            keep = {r: b for r, b in self.bufs.items() if not r & mask}
            send = {r: self.bufs[r ^ mask] for r in keep}
        else:
            own = bit(axis, mask)
            pre = higher(rest, mask)
            keep, send = {}, {}
            for r, b in self.bufs.items():
                parts = b.reshape((pre, 2, b.shape[0] // (2 * pre)) + b.shape[1:])
                send[r], keep[r] = (
                    lax.dynamic_index_in_dim(parts, i, 1, keepdims=False).reshape(
                        (-1,) + b.shape[1:]
                    )
                    for i in (1 - own, own)
                )
        got = {}
        first = []
        for r, b in send.items():
            b = after(b, *others) if others else b
            if pieces == 1:
                got[r] = swap(b, axis, mask)
                first.append(got[r])
                continue
            half = b.shape[0] // 2
            lower = swap(b[:half], axis, mask)
            upper = swap(after(b[half:], lower), axis, mask)
            got[r] = jnp.concatenate([lower, upper])
            first.append(lower)
        self.bufs = {}
        for r in keep:
            other = after(got[r], *hold) if hold else got[r]
            total = keep[r].astype(f32) + other.astype(f32)
            self.bufs[r] = total.astype(b16) if rest else total
        self.done += 1
        return first

    def finish(self):
        while self.done < len(self.order):
            self.step()
        return self.bufs[0][0]


def shift_outer(values, by):
    size = lax.axis_size("ctx")
    return lax.ppermute(
        values, "ctx", [(i, i + 2 * by) for i in range(size) if 0 <= i + 2 * by < size]
    )


def dot(a, b, dims):
    return lax.dot_general(a, b, (dims, ((), ())), preferred_element_type=f32)


def fill_bias(blocks, tokens, place, seg_refs, bias):
    queries = jnp.broadcast_to(seg_refs[0][0:1, :].astype(f32), (tokens, tokens))
    for j in range(blocks):
        keys = jnp.broadcast_to(seg_refs[j][0:1, :].astype(f32), (tokens, tokens)).T
        allowed = (keys == queries) & (place >= j)
        if j == 0:
            key_row = lax.broadcasted_iota(jnp.int32, (tokens, tokens), 0)
            query_col = lax.broadcasted_iota(jnp.int32, (tokens, tokens), 1)
            allowed = allowed & (key_row <= query_col)
        bias[j * tokens : (j + 1) * tokens, :] = jnp.where(allowed, 0.0, masked)


def heads_side(ref):
    return jnp.concatenate(
        [ref[h * HEAD_DIM : (h + 1) * HEAD_DIM, :] for h in range(GROUP)], axis=1
    )


def forward_kernel(blocks, tokens, place_ref, *refs):
    q_ref = refs[0]
    k_refs = refs[1 : 1 + blocks]
    v_refs = refs[1 + blocks : 1 + 2 * blocks]
    seg_refs = refs[1 + 2 * blocks : 1 + 3 * blocks]
    att_ref, lse_ref, bias = refs[1 + 3 * blocks :]

    @pl.when(pl.program_id(1) == 0)
    def _():
        fill_bias(blocks, tokens, place_ref[0], seg_refs, bias)

    keys = jnp.concatenate([r[...] for r in k_refs], axis=1)
    values = jnp.concatenate([r[...] for r in v_refs], axis=1)
    scores = dot(keys, heads_side(q_ref), ((0,), (0,)))
    for h in range(GROUP):
        own = scores[:, h * tokens : (h + 1) * tokens] + bias[...]
        top = jnp.max(own, axis=0, keepdims=True)
        probs = jnp.exp(own - top)
        total = jnp.sum(probs, axis=0, keepdims=True)
        out = dot(values, probs.astype(b16), ((1,), (0,)))
        att_ref[h * HEAD_DIM : (h + 1) * HEAD_DIM, :] = (out / total).astype(b16)
        lse_ref[0, h : h + 1, :] = top + jnp.log(total)


def backward_kernel(blocks, tokens, place_ref, *refs):
    q_ref, datt_ref, lse_ref = refs[:3]
    k_refs = refs[3 : 3 + blocks]
    v_refs = refs[3 + blocks : 3 + 2 * blocks]
    seg_refs = refs[3 + 2 * blocks : 3 + 3 * blocks]
    dq_ref = refs[3 + 3 * blocks]
    dkv_refs = refs[4 + 3 * blocks : 4 + 4 * blocks]
    bias, p_scr, ds_scr = refs[4 + 4 * blocks :]

    @pl.when(pl.program_id(1) == 0)
    def _():
        fill_bias(blocks, tokens, place_ref[0], seg_refs, bias)

    keys = jnp.concatenate([r[...] for r in k_refs], axis=1)
    values = jnp.concatenate([r[...] for r in v_refs], axis=1)
    queries = heads_side(q_ref)
    grads = heads_side(datt_ref)
    scores = dot(keys, queries, ((0,), (0,)))
    d_probs = dot(values, grads, ((0,), (0,)))
    for h in range(GROUP):
        lanes = slice(h * tokens, (h + 1) * tokens)
        probs = jnp.exp(scores[:, lanes] + bias[...] - lse_ref[0, h : h + 1, :])
        weighted = probs * d_probs[:, lanes]
        delta = jnp.sum(weighted, axis=0, keepdims=True)
        p_scr[:, lanes] = probs.astype(b16)
        ds_scr[:, lanes] = (weighted - probs * delta).astype(b16)
    d_scores = ds_scr[...]
    dq = dot(keys, d_scores, ((1,), (0,)))
    for h in range(GROUP):
        dq_ref[h * HEAD_DIM : (h + 1) * HEAD_DIM, :] = dq[:, h * tokens : (h + 1) * tokens]
    dk = dot(queries, d_scores, ((1,), (1,)))
    dv = dot(grads, p_scr[...], ((1,), (1,)))
    for j in range(blocks):
        lanes = slice(j * tokens, (j + 1) * tokens)
        dkv_refs[j][0] = dk[:, lanes].astype(b16)
        dkv_refs[j][1] = dv[:, lanes].astype(b16)


def kv_specs(blocks, tokens):
    per_group = (HEAD_DIM, tokens)
    key = pl.BlockSpec(per_group, lambda s, g, _: (g, s))
    value = pl.BlockSpec(per_group, lambda s, g, _: (KEY_VALUE_HEADS + g, s))
    seg_row = 2 * KEY_VALUE_HEADS * HEAD_DIM // 16
    seg = pl.BlockSpec((16, tokens), lambda s, g, _: (seg_row, s))
    return [key] * blocks + [value] * blocks + [seg] * blocks


def attend(place, q_rot, pieces, sequences, tokens):
    blocks = len(pieces)
    heads = pl.BlockSpec((GROUP * HEAD_DIM, tokens), lambda s, g, _: (g, s))
    stat = pl.BlockSpec((1, 8, tokens), lambda s, g, _: (g, 0, s))
    wide = sequences * tokens
    return pl.pallas_call(
        functools.partial(forward_kernel, blocks, tokens),
        grid_spec=pltpu.PrefetchScalarGridSpec(
            num_scalar_prefetch=1,
            grid=(sequences, KEY_VALUE_HEADS),
            in_specs=[heads] + kv_specs(blocks, tokens),
            out_specs=[heads, stat],
            scratch_shapes=[pltpu.VMEM((blocks * tokens, tokens), f32)],
        ),
        out_shape=[
            jax.ShapeDtypeStruct((QUERY_HEADS * HEAD_DIM, wide), b16),
            jax.ShapeDtypeStruct((KEY_VALUE_HEADS, 8, wide), f32),
        ],
        compiler_params=pltpu.CompilerParams(vmem_limit_bytes=40 << 20),
        cost_estimate=pl.CostEstimate(flops=1, bytes_accessed=1, transcendentals=0),
        name="attend",
    )(place, q_rot, *pieces, *pieces, *pieces)


def attend_back(place, q_rot, datt, lse, pieces, sequences, tokens):
    blocks = len(pieces)
    heads = pl.BlockSpec((GROUP * HEAD_DIM, tokens), lambda s, g, _: (g, s))
    stat = pl.BlockSpec((1, 8, tokens), lambda s, g, _: (g, 0, s))
    pair = pl.BlockSpec((2, HEAD_DIM, tokens), lambda s, g, _: (0, g, s))
    wide = sequences * tokens
    return pl.pallas_call(
        functools.partial(backward_kernel, blocks, tokens),
        grid_spec=pltpu.PrefetchScalarGridSpec(
            num_scalar_prefetch=1,
            grid=(sequences, KEY_VALUE_HEADS),
            in_specs=[heads, heads, stat] + kv_specs(blocks, tokens),
            out_specs=[heads] + [pair] * blocks,
            scratch_shapes=[
                pltpu.VMEM((blocks * tokens, tokens), f32),
                pltpu.VMEM((blocks * tokens, GROUP * tokens), b16),
                pltpu.VMEM((blocks * tokens, GROUP * tokens), b16),
            ],
        ),
        out_shape=[jax.ShapeDtypeStruct((QUERY_HEADS * HEAD_DIM, wide), f32)]
        + [jax.ShapeDtypeStruct((2, KEY_VALUE_HEADS * HEAD_DIM, wide), b16)] * blocks,
        compiler_params=pltpu.CompilerParams(vmem_limit_bytes=48 << 20),
        cost_estimate=pl.CostEstimate(flops=1, bytes_accessed=1, transcendentals=0),
        name="attend_back",
    )(place, q_rot, datt, lse, *pieces, *pieces, *pieces)


def turned(low, high, cosine, sine, sign):
    return low * cosine - sign * high * sine, high * cosine + sign * low * sine


def turn_rows(source, target, heads, cosine, sine, sign, scale):
    for h in range(heads):
        at = h * HEAD_DIM
        low, high = source[at : at + HALF], source[at + HALF : at + HEAD_DIM]
        pair = turned(low, high, cosine, sine, sign)
        for i, half in enumerate(pair):
            rows = slice(at + i * HALF, at + (i + 1) * HALF)
            target[rows] = (half * scale).astype(target.dtype)


def project_kv_kernel(parts, kv_cols, ctx, *refs):
    x_ref, inv_ref, gain_ref = refs[:3]
    w_refs = refs[3 : 3 + parts]
    seg_ref, cos_ref, sin_ref, normed_ref, own_ref, blocks, flat = refs[3 + parts :]
    for r in range(parts):
        normed = (x_ref[r].astype(f32) * inv_ref[...] * gain_ref[r]).astype(b16)
        normed_ref[r] = normed
        part = dot(w_refs[r][...], normed, ((1,), (0,)))
        if r == 0:
            blocks[...] = part
        else:
            blocks[...] += part
    rows = blocks.shape[0] // ctx
    kv_width = KEY_VALUE_HEADS * HEAD_DIM
    for c in range(ctx):
        base, at = c * rows, c * kv_cols
        flat[at : at + kv_cols] = blocks[base : base + kv_cols]
        at += kv_width
        flat[at : at + kv_cols] = blocks[base + kv_cols : base + 2 * kv_cols]
    turn_rows(flat, own_ref, KEY_VALUE_HEADS, cos_ref[...], sin_ref[...], 1.0, 1.0)
    own_ref[kv_width : 2 * kv_width] = flat[kv_width : 2 * kv_width].astype(b16)
    own_ref[2 * kv_width : 2 * kv_width + 16] = seg_ref[...]


def project_q_kernel(parts, scale, normed_ref, cos_ref, sin_ref, *refs):
    w_refs = refs[:parts]
    q_ref, flat = refs[parts:]
    acc = dot(w_refs[0][...], normed_ref[0], ((1,), (0,)))
    for r in range(1, parts):
        acc = acc + dot(w_refs[r][...], normed_ref[r], ((1,), (0,)))
    flat[...] = acc
    turn_rows(flat, q_ref, QUERY_HEADS, cos_ref[...], sin_ref[...], 1.0, scale)


def project_q_back_kernel(parts, scale, dq_ref, normed_ref, cos_ref, sin_ref, *refs):
    w_refs = refs[:parts]
    dn_ref = refs[parts]
    g_refs = refs[1 + parts : 1 + 2 * parts]
    flat = refs[1 + 2 * parts]
    turn_rows(dq_ref, flat, QUERY_HEADS, cos_ref[...], sin_ref[...], -1.0, scale)
    for r in range(parts):
        g_refs[r][...] = dot(flat[...], normed_ref[r], ((1,), (1,))).astype(b16)
    for r in range(parts):
        dn_ref[r] = dot(w_refs[r][...], flat[...], ((0,), (0,)))


def project_kv_back_kernel(parts, kv_cols, ctx, me_ref, *refs):
    dkv_ref, cos_ref, sin_ref, normed_ref, dn_q_ref, x_ref, inv_ref, gain_ref, d_mid_ref = refs[:9]
    w_refs = refs[9 : 9 + parts]
    out_ref, g_gain_ref = refs[9 + parts : 11 + parts]
    g_refs = refs[11 + parts : 11 + 2 * parts]
    flat, blocks, d_x = refs[11 + 2 * parts :]
    kv_width = KEY_VALUE_HEADS * HEAD_DIM
    turn_rows(dkv_ref.at[0], flat, KEY_VALUE_HEADS, cos_ref[...], sin_ref[...], -1.0, 1.0)
    rows = blocks.shape[0] // ctx
    for c in range(ctx):
        base, at = c * rows, c * kv_cols
        blocks[base : base + kv_cols] = flat[at : at + kv_cols]
        blocks[base + kv_cols : base + 2 * kv_cols] = dkv_ref[1, at : at + kv_cols]
        blocks[base + 2 * kv_cols : base + rows] = jnp.zeros(
            (rows - 2 * kv_cols, blocks.shape[1]), f32
        )
    low = blocks[...].astype(b16)
    for r in range(parts):
        g_refs[r][...] = dot(low, normed_ref[r], ((1,), (1,))).astype(b16)
    inv = inv_ref[...]
    mean = jnp.zeros_like(inv)
    for r in range(parts):
        d_normed = dn_q_ref[r] + dot(w_refs[r][...], low, ((0,), (0,)))
        x = x_ref[r].astype(f32)
        g_gain_ref[r] = jnp.sum(d_normed * (x * inv), axis=1, keepdims=True)
        scaled = d_normed * gain_ref[r]
        d_x[r] = scaled
        mean = mean + jnp.sum(scaled * x, axis=0, keepdims=True)
    mean = mean / (parts * x_ref.shape[1]) * (inv * inv * inv)
    features, tokens = x_ref.shape[1], out_ref.shape[2]
    for d in range(parts):
        r = me_ref[0] ^ d
        total = d_mid_ref[d] + inv * d_x[r] - x_ref[r].astype(f32) * mean
        for s in range(out_ref.shape[0]):
            lanes = slice(s * tokens, (s + 1) * tokens)
            out_ref[s, d * features : (d + 1) * features] = total[:, lanes].astype(b16)


def mix_kernel(parts, me_ref, att_ref, x_ref, gain_ref, *refs):
    w_refs = refs[:parts]
    mid_ref, inv_ref, normed_ref, normed_t_ref = refs[parts:]
    mid = x_ref[...].astype(f32)
    for r in range(parts):
        mid = mid + dot(att_ref[me_ref[0] ^ r], w_refs[r][...], ((0,), (1,)))
    mid_ref[...] = mid
    inv = lax.rsqrt(jnp.mean(mid * mid, axis=-1, keepdims=True) + epsilon)
    inv_ref[...] = inv
    normed = mid * inv * gain_ref[...]
    rows = normed_ref.shape[2]
    for d in range(parts):
        part = normed[:, d * rows : (d + 1) * rows]
        normed_ref[me_ref[0] ^ d] = part.astype(b16)
        normed_t_ref[me_ref[0] ^ d] = part.T.astype(b16)


def mix_back_kernel(parts, me_ref, att_ref, cot_ref, mid_ref, inv_ref, gain_ref, dn_ref, *refs):
    w_refs = refs[:parts]
    datt_ref, d_mid_ref, g_gain_ref = refs[parts : 3 + parts]
    g_refs = refs[3 + parts : 3 + 2 * parts]
    flipped = refs[3 + 2 * parts]
    rows = dn_ref.shape[2]
    inv = inv_ref[...]
    mean = jnp.zeros_like(inv)
    for d in range(parts):
        lanes = slice(d * rows, (d + 1) * rows)
        d_normed = dn_ref[me_ref[0] ^ d]
        mid = mid_ref[:, lanes]
        g_gain_ref[d] = jnp.sum(d_normed * (mid * inv), axis=0, keepdims=True)
        mean = mean + jnp.sum(d_normed * gain_ref[:, lanes] * mid, axis=-1, keepdims=True)
    mean = mean / (parts * rows) * (inv * inv * inv)
    for d in range(parts):
        lanes = slice(d * rows, (d + 1) * rows)
        scaled = dn_ref[me_ref[0] ^ d] * gain_ref[:, lanes]
        d_mid = (inv * scaled - mid_ref[:, lanes] * mean).T
        cot = [cot_ref[s, lanes].astype(f32) for s in range(cot_ref.shape[0])]
        d_mid = d_mid + jnp.concatenate(cot, axis=1)
        d_mid_ref[d] = d_mid
        flipped[lanes] = d_mid.astype(b16)
    for r in range(parts):
        at = me_ref[0] ^ r
        g_refs[r][...] = dot(flipped[...], att_ref[at], ((1,), (1,))).astype(b16)
        datt_ref[at] = dot(w_refs[r][...], flipped[...], ((0,), (0,))).astype(b16)


def ffn_kernel(parts, per, me_ref, n_ref, nt_ref, cot_ref, mid_ref, *refs):
    f_refs = [refs[:parts], refs[parts : 2 * parts]]
    d_refs = refs[2 * parts : 3 * parts]
    out_ref, dn_ref = refs[3 * parts : 3 * parts + 2]
    rest = refs[3 * parts + 2 :]
    gf_refs = [rest[:parts], rest[parts : 2 * parts]]
    gd_refs = rest[2 * parts : 3 * parts]
    acc, down, g_down, hidden, cot_t, cot = rest[3 * parts :]
    step = pl.program_id(0)
    for r in range(parts):

        @pl.when(step == r)
        def _(r=r):
            down[...] = d_refs[r][...]

    @pl.when(step == 0)
    def _():
        acc[...] = jnp.zeros_like(acc)
        length = cot_ref.shape[2]
        for s in range(cot_ref.shape[0]):
            cot_t[:, s * length : (s + 1) * length] = cot_ref[s]
            cot[s * length : (s + 1) * length, :] = cot_ref[s].T
        dn_ref[...] = jnp.zeros_like(dn_ref)

    cut = f_refs[0][0].shape[2]
    ff = (cut + f_refs[1][0].shape[2]) // 2
    d_hidden = dot(cot[...], down[...], ((1,), (0,)))
    for i in range(per):
        both = []
        for side in f_refs:
            part = dot(n_ref[0], side[0][i], ((1,), (0,)))
            for r in range(1, parts):
                part = part + dot(n_ref[r], side[r][i], ((1,), (0,)))
            both.append(part)
        both = jnp.concatenate(both, axis=1)
        gate, up = both[:, :ff], both[:, ff:]
        grad = d_hidden[:, i * ff : (i + 1) * ff]
        sigma = jax.nn.sigmoid(gate)
        silu = gate * sigma
        hidden[:, i * ff : (i + 1) * ff] = (silu * up).astype(b16)
        d_gate = grad * up * (sigma * (1.0 + gate * (1.0 - sigma)))
        d_both = jnp.concatenate([d_gate, grad * silu], axis=1).astype(b16)
        sides = (d_both[:, :cut], d_both[:, cut:])
        for r in range(parts):
            for side in range(2):
                grad = dot(nt_ref[r], sides[side], ((1,), (0,)))
                gf_refs[side][r][i] = grad.astype(b16)
            dn_ref[r] += dot(sides[0], f_refs[0][r][i], ((1,), (1,))) + dot(
                sides[1], f_refs[1][r][i], ((1,), (1,))
            )
    acc[...] += dot(hidden[...], down[...], ((1,), (1,)))
    g_down[...] = dot(cot_t[...], hidden[...], ((1,), (0,))).astype(b16)
    for r in range(parts):

        @pl.when(step == r)
        def _(r=r):
            gd_refs[r][...] = g_down[...]

    @pl.when(step == parts - 1)
    def _():
        length = out_ref.shape[2]
        for s in range(out_ref.shape[0]):
            part = slice(s * length, (s + 1) * length)
            out_ref[s] = (mid_ref[part] + acc[part]).T.astype(b16)


def ffn(me, n_rel, nt_rel, cot, mid, f_one, f_two, d_list):
    parts = len(f_one)
    ctx, rows, cut = f_one[0].shape
    wide = cut + f_two[0].shape[2]
    per = ctx // parts
    tokens, width = mid.shape
    down_shape = d_list[0].shape

    def whole(a):
        return pl.BlockSpec(a.shape, lambda i, me: (0,) * a.ndim, pipeline_mode=pl.Buffered(1))

    f_specs = [
        pl.BlockSpec((per, rows, n), lambda i, me: (me[0] ^ i, 0, 0))
        for n in [cut] * parts + [wide - cut] * parts
    ]
    out_shape = [
        jax.ShapeDtypeStruct(cot.shape, b16),
        jax.ShapeDtypeStruct((parts, tokens, rows), f32),
    ]
    out_shape += [jax.ShapeDtypeStruct(f.shape, b16) for f in f_one + f_two]
    out_shape += [jax.ShapeDtypeStruct(down_shape, b16)] * parts
    return pl.pallas_call(
        functools.partial(ffn_kernel, parts, per),
        grid_spec=pltpu.PrefetchScalarGridSpec(
            num_scalar_prefetch=1,
            grid=(parts,),
            in_specs=[whole(a) for a in (n_rel, nt_rel, cot, mid)]
            + f_specs
            + [whole(a) for a in d_list],
            out_specs=[whole(a) for a in out_shape[:2]]
            + f_specs
            + [whole(a) for a in d_list],
            scratch_shapes=[
                pltpu.VMEM((tokens, width), f32),
                pltpu.VMEM(down_shape, b16),
                pltpu.VMEM(down_shape, b16),
                pltpu.VMEM((tokens, per * wide // 2), b16),
                pltpu.VMEM((width, tokens), b16),
                pltpu.VMEM((tokens, width), b16),
            ],
        ),
        out_shape=out_shape,
        compiler_params=pltpu.CompilerParams(vmem_limit_bytes=58 << 20),
        cost_estimate=pl.CostEstimate(flops=1, bytes_accessed=1, transcendentals=0),
        name="ffn",
    )(me, n_rel, nt_rel, cot, mid, *f_one, *f_two, *d_list)


def in_vmem(kernel, name, out_shape, scratch, *args, scalars=0):
    vmem = pl.BlockSpec(memory_space=pltpu.VMEM)
    smem = pl.BlockSpec(memory_space=pltpu.SMEM)
    return pl.pallas_call(
        kernel,
        in_specs=[smem] * scalars + [vmem] * (len(args) - scalars),
        out_specs=[vmem] * len(out_shape),
        out_shape=out_shape,
        scratch_shapes=scratch,
        compiler_params=pltpu.CompilerParams(vmem_limit_bytes=48 << 20),
        cost_estimate=pl.CostEstimate(flops=1, bytes_accessed=1, transcendentals=0),
        name=name,
    )(*args)


def per_device(
    inputs,
    gain_one,
    query_weight,
    key_weight,
    value_weight,
    output_weight,
    gain_two,
    gate_weight,
    up_weight,
    down_weight,
    segment_ids,
    cotangent,
):
    dp, ctx = lax.axis_size("dp"), lax.axis_size("ctx")
    sequences, tokens, width = inputs.shape
    total = sequences * tokens
    rows = query_weight.shape[0]
    q_cols, kv_cols = query_weight.shape[1], key_weight.shape[1]
    ff_cols = gate_weight.shape[1]
    down_rows, out_cols = down_weight.shape
    kv_width = KEY_VALUE_HEADS * HEAD_DIM
    shape_of = jax.ShapeDtypeStruct

    dp_bits, ctx_bits = bits_of("dp", dp), bits_of("ctx", ctx)
    x_last = ctx_bits + dp_bits
    y_last = ctx_bits[:-1] + dp_bits[:-1] + ctx_bits[-1:] + dp_bits[-1:]
    z_last = ctx_bits[:-2] + ctx_bits[-1:] + dp_bits[:-1] + ctx_bits[-2:-1] + dp_bits[-1:]

    place = lax.axis_index("ctx")
    me = lax.axis_index("dp")
    me_arg = me.reshape(1).astype(jnp.int32)
    place_arg = place.reshape(1).astype(jnp.int32)

    def relative(stacked):
        return jnp.stack(
            [lax.dynamic_index_in_dim(stacked, me ^ r, 0, keepdims=False) for r in range(dp)]
        )

    gains = jnp.concatenate([gain_one, gain_two])
    gain_rows = -(-gains.size // rows)
    gains = jnp.pad(gains, (0, gain_rows * rows - gains.size)).reshape(gain_rows, rows)
    pad_rows = -(2 * kv_cols + gain_rows) % 8
    kv_block = jnp.concatenate(
        [key_weight.T, value_weight.T, gains, jnp.zeros((pad_rows, rows), b16)]
    )
    kv_gather = Gather(kv_block, y_last)
    qo_gather = Gather(jnp.concatenate([query_weight.T, output_weight.T]), x_last)
    gate_up = jnp.concatenate([gate_weight, up_weight], axis=1)
    cut = max(2 * ff_cols * 3 // 5 // 128, 1) * 128
    one_gather = Gather(gate_up[:, :cut], x_last)
    two_gather = Gather(gate_up[:, cut:], y_last)
    down_gather = Gather(down_weight.T, z_last)
    outer = len(ctx_bits) - 1
    token = kv_gather.step()
    one_gather.step(*token)
    two_gather.step(*token)
    token = kv_gather.step()
    down_gather.step(*token)
    qo_gather.step(*token)
    while kv_gather.done < len(x_last) - 1:
        token = kv_gather.step()
    for _ in range(outer - 1):
        two_gather.step(*token)
        down_gather.step(*token)
        one_gather.step(*token)
        qo_gather.step(*token)
    kv_gather.step()
    kv_all = kv_gather.result()

    first_gain = 2 * kv_cols
    gain_all = kv_all[0][:, first_gain : first_gain + gain_rows].reshape(ctx, -1)
    gain_part = gain_one.shape[0]
    gain_a = relative(gain_all[:, :gain_part].reshape(dp, rows, 1).astype(f32))
    gain_b = gain_all[:, gain_part : 2 * gain_part].reshape(1, width).astype(f32)
    kv_all = [a.reshape(-1, rows) for a in kv_all]

    cot = jnp.transpose(cotangent, (0, 2, 1))
    x_low = inputs.reshape(total, width)
    x = x_low.astype(f32)
    inv_one = lax.rsqrt(jnp.mean(x * x, axis=-1) + epsilon).reshape(1, total)
    x_t = relative(x_low.T.reshape(dp, rows, total))
    positions = (place * tokens + jnp.arange(tokens, dtype=jnp.int32)).astype(f32)
    positions = jnp.tile(positions, sequences)
    frequency = jnp.exp(jnp.arange(HALF, dtype=f32) * (-2.0 * math.log(rope_base) / HEAD_DIM))
    angles = frequency[:, None] * positions[None, :]
    cosine, sine = jnp.cos(angles), jnp.sin(angles)
    score_scale = HEAD_DIM ** (-0.5)
    seg_row = jnp.pad(segment_ids.reshape(1, total).astype(b16), ((0, 15), (0, 0)))
    block_rows = kv_all[0].shape[0]
    one_t, own = in_vmem(
        functools.partial(project_kv_kernel, dp, kv_cols, ctx),
        "project_kv",
        [shape_of((dp, rows, total), b16), shape_of((2 * kv_width + 16, total), b16)],
        [pltpu.VMEM((block_rows, total), f32), pltpu.VMEM((2 * kv_width, total), f32)],
        x_t,
        inv_one,
        gain_a,
        *kv_all,
        seg_row,
        cosine,
        sine,
    )

    steps = ctx // 4
    inner = bit("ctx", 1)
    straight = [own]
    for _ in range(steps):
        straight.append(shift_outer(straight[-1], 1))
    crossed = [
        swap(jnp.where(inner == 0, straight[k], straight[k + 1]), "ctx", 1) for k in range(steps)
    ]
    while two_gather.done < len(x_last) - 2:
        spread = two_gather.step()
    while down_gather.done < len(x_last) - 2:
        spread += down_gather.step()
    while one_gather.done < outer + 1:
        one_gather.step()
    while qo_gather.done < outer + 1:
        qo_gather.step()
    ahead = qo_gather.step(*spread)
    while qo_gather.done < len(x_last):
        qo_gather.step()
    q_all = [a[:, :q_cols].reshape(-1, rows) for a in qo_gather.result()]
    out_all = [a[:, q_cols:].reshape(-1, rows) for a in qo_gather.result()]
    (q_rot,) = in_vmem(
        functools.partial(project_q_kernel, dp, score_scale),
        "project_q",
        [shape_of((width, total), b16)],
        [pltpu.VMEM((width, total), f32)],
        after(one_t, straight[1]),
        cosine,
        sine,
        *q_all,
    )
    one_gather.step(*ahead, straight[1])
    down_gather.step(straight[steps])
    two_gather.step(*crossed)
    pieces = []
    for k in range(steps):
        pieces += [straight[k], crossed[k]]
    pieces.append(straight[steps])

    att, lse = attend(place_arg, q_rot, pieces, sequences, tokens)
    for g in (one_gather, two_gather, down_gather):
        while g.done < len(x_last):
            g.step(lse)
    down_all = [a.reshape(-1, down_rows) for a in down_gather.result()]
    att_3 = att.reshape(dp, rows, total)

    mid, inv_two, two, two_t = in_vmem(
        functools.partial(mix_kernel, dp),
        "mix",
        [
            shape_of((total, width), f32),
            shape_of((total, 1), f32),
            shape_of((dp, total, rows), b16),
            shape_of((dp, rows, total), b16),
        ],
        [],
        me_arg,
        att_3,
        x_low,
        gain_b,
        *out_all,
        scalars=1,
    )
    output, d_two, *grads = ffn(me_arg, two, two_t, cot, mid, one_gather.result(), two_gather.result(), down_all)
    g_one = Scatter(grads[:dp], x_last[::-1])
    g_two = Scatter(grads[dp : 2 * dp], y_last[::-1])
    g_down = Scatter([g.reshape(ctx, out_cols, down_rows) for g in grads[2 * dp :]], z_last[::-1])
    d_att, d_mid, g_gain_two, *g_out = in_vmem(
        functools.partial(mix_back_kernel, dp),
        "mix_back",
        [
            shape_of(att_3.shape, b16),
            shape_of((dp, rows, total), f32),
            shape_of((dp, 1, rows), f32),
        ]
        + [shape_of((width, rows), b16)] * dp,
        [pltpu.VMEM((width, total), b16)],
        me_arg,
        att_3,
        cot,
        mid,
        inv_two,
        gain_b,
        d_two,
        *out_all,
        scalars=1,
    )
    folded = g_one.step(hold=(d_att,))
    folded += [t for g in (g_two, g_down) for t in g.step(hold=(d_att, *folded[:1]))]
    d_att = after(d_att.reshape(width, total), *folded)
    under_x, under_y, under_z = g_one.step(), g_two.step(), g_down.step()
    dq_rot, *parts = attend_back(place_arg, q_rot, d_att, lse, pieces, sequences, tokens)
    dq_rot = after(dq_rot, *under_x, *under_y, *under_z)
    parts = [after(p, *under_y) for p in parts]
    dn_q, *g_q = in_vmem(
        functools.partial(project_q_back_kernel, dp, score_scale),
        "project_q_back",
        [shape_of((dp, rows, total), f32)] + [shape_of((width, rows), b16)] * dp,
        [pltpu.VMEM((width, total), b16)],
        dq_rot,
        one_t,
        cosine,
        sine,
        *q_all,
    )

    returned = [swap(parts[2 * k + 1], "ctx", 1).astype(f32) for k in range(steps)]
    here = []
    for k in range(steps + 1):
        value = parts[2 * k].astype(f32)
        if k < steps:
            value = value + jnp.where(inner == 0, returned[k], 0.0)
        if k > 0:
            value = value + jnp.where(inner == 1, returned[k - 1], 0.0)
        here.append(value)
    carried = after(here[steps], *under_x, *under_z)
    for k in range(steps, 0, -1):
        moved = shift_outer(carried.astype(b16), -1)
        if k == steps:
            first_moved = moved
        carried = here[k - 1] + moved.astype(f32)
    g_qo = [
        jnp.concatenate([q.reshape(ctx, q_cols, rows), o.reshape(ctx, out_cols, rows)], axis=1)
        for q, o in zip(g_q, g_out, strict=True)
    ]
    g_qo = Scatter(g_qo, x_last[::-1])
    g_qo.step(parts[0])
    beside = g_two.step(hold=(first_moved,)) + g_down.step(hold=(first_moved,))
    beside += g_one.step(*returned)
    ahead = g_qo.step(*beside[:2])
    for g in (g_two, g_down):
        g.step(first_moved)
    carried = after(carried, *beside)
    input_grad, g_gain_one, *g_kv = in_vmem(
        functools.partial(project_kv_back_kernel, dp, kv_cols, ctx),
        "project_kv_back",
        [shape_of((sequences, width, tokens), b16), shape_of((dp, rows, 1), f32)]
        + [shape_of((block_rows, rows), b16)] * dp,
        [
            pltpu.VMEM((kv_width, total), f32),
            pltpu.VMEM((block_rows, total), f32),
            pltpu.VMEM((dp, rows, total), f32),
        ],
        me_arg,
        carried,
        cosine,
        sine,
        one_t,
        dn_q,
        x_t,
        inv_one,
        gain_a,
        d_mid,
        *kv_all,
        scalars=1,
    )
    g_gains = jnp.concatenate(
        [relative(g_gain_one).reshape(ctx, gain_part), g_gain_two.reshape(ctx, gain_part)], axis=1
    ).astype(b16)
    g_gains = jnp.pad(g_gains, ((0, 0), (0, gain_rows * rows - 2 * gain_part)))
    g_gains = jnp.pad(g_gains.reshape(ctx, gain_rows, rows), ((0, 0), (0, pad_rows), (0, 0)))
    g_kv = [
        jnp.concatenate([g.reshape(ctx, -1, rows)[:, :first_gain], g_gains], axis=1) for g in g_kv
    ]
    g_kv = Scatter(g_kv, x_last[::-1])
    g_one.step(first_moved, hold=(input_grad,))
    token = g_kv.step(*ahead)
    g_qo.step()
    for g in (g_two, g_down, g_one):
        while g.done < len(x_last):
            g.step(hold=(input_grad,))
    while g_kv.done < len(x_last):
        token = g_kv.step(*token)
        if g_qo.done < min(g_kv.done, len(x_last)):
            g_qo.step(*token)
    g_kv, g_qo, g_down = g_kv.finish(), g_qo.finish(), g_down.finish()
    g_gu = jnp.concatenate([g_one.finish(), g_two.finish()], axis=1)
    g_gains = g_kv[first_gain : first_gain + gain_rows].reshape(-1)
    return (
        jnp.transpose(output, (0, 2, 1)),
        jnp.transpose(input_grad, (0, 2, 1)),
        g_gains[:gain_part],
        g_qo[:q_cols].T,
        g_kv[:kv_cols].T,
        g_kv[kv_cols : 2 * kv_cols].T,
        g_qo[q_cols:].T,
        g_gains[gain_part : 2 * gain_part],
        g_gu[:, :ff_cols],
        g_gu[:, ff_cols:],
        g_down.T,
    )


def solution(mesh):
    act = P("dp", "ctx", None)
    weight = P("dp", "ctx")
    gain = P("ctx")
    return jax.shard_map(
        per_device,
        mesh=mesh,
        in_specs=(
            act, gain, weight, weight, weight, weight, gain, weight, weight, weight, P("dp", "ctx"), act,
        ),
        out_specs=(
            act, act, gain, weight, weight, weight, weight, gain, weight, weight, weight,
        ),
        check_vma=False,
    )
```

```python
import functools
import math

import jax
import jax.numpy as jnp
from jax import lax
from jax.experimental import pallas as pl
from jax.experimental.pallas import tpu as pltpu
from jax.sharding import PartitionSpec as P

QUERY_HEADS = 15
KEY_VALUE_HEADS = 5
HEAD_DIM = 64
GROUP = QUERY_HEADS // KEY_VALUE_HEADS
HALF = HEAD_DIM // 2

epsilon = 1e-05
rope_base = 10000.0
masked = -1e30
f32 = jnp.float32
b16 = jnp.bfloat16


def bits_of(axis, size):
    masks = []
    mask = size // 2
    while mask:
        masks.append((axis, mask))
        mask //= 2
    return masks


def swap(values, axis, mask):
    size = lax.axis_size(axis)
    return lax.ppermute(values, axis, [(i, i ^ mask) for i in range(size)])


def bit(axis, mask):
    return (lax.axis_index(axis) // mask) % 2


def after(values, *others):
    return lax.optimization_barrier((values, *others))[0]


def higher(order, mask):
    return 2 ** sum(1 for axis, m in order if axis == "ctx" and m > mask)


class Gather:
    def __init__(self, block, order):
        self.bufs = {0: block[None]}
        self.order = order
        self.done = 0

    def step(self, *others, hold=()):
        axis, mask = self.order[self.done]
        sent = {r: after(b, *others) if others else b for r, b in self.bufs.items()}
        got = {r: swap(b, axis, mask) for r, b in sent.items()}
        if hold:
            got = {r: after(b, *hold) for r, b in got.items()}
        if axis == "dp":
            self.bufs = {**self.bufs, **{r ^ mask: b for r, b in got.items()}}
        else:
            upper = bit(axis, mask) == 1
            pre = higher(self.order[: self.done], mask)
            for r, theirs in got.items():
                mine = self.bufs[r]
                shape = (pre, 1, mine.shape[0] // pre) + mine.shape[1:]
                mine, theirs = mine.reshape(shape), theirs.reshape(shape)
                both = jnp.concatenate(
                    [jnp.where(upper, theirs, mine), jnp.where(upper, mine, theirs)], axis=1
                )
                self.bufs[r] = both.reshape((-1,) + shape[3:])
        self.done += 1
        return list(got.values())

    def result(self):
        return [self.bufs[r] for r in sorted(self.bufs)]


class Scatter:
    def __init__(self, bufs, order):
        self.bufs = dict(enumerate(bufs))
        self.order = order
        self.done = 0

    def step(self, *others, pieces=1, hold=()):
        axis, mask = self.order[self.done]
        rest = self.order[self.done + 1 :]
        if axis == "dp":
            keep = {r: b for r, b in self.bufs.items() if not r & mask}
            send = {r: self.bufs[r ^ mask] for r in keep}
        else:
            own = bit(axis, mask)
            pre = higher(rest, mask)
            keep, send = {}, {}
            for r, b in self.bufs.items():
                parts = b.reshape((pre, 2, b.shape[0] // (2 * pre)) + b.shape[1:])
                send[r], keep[r] = (
                    lax.dynamic_index_in_dim(parts, i, 1, keepdims=False).reshape(
                        (-1,) + b.shape[1:]
                    )
                    for i in (1 - own, own)
                )
        got = {}
        first = []
        for r, b in send.items():
            b = after(b, *others) if others else b
            if pieces == 1:
                got[r] = swap(b, axis, mask)
                first.append(got[r])
                continue
            half = b.shape[0] // 2
            lower = swap(b[:half], axis, mask)
            upper = swap(after(b[half:], lower), axis, mask)
            got[r] = jnp.concatenate([lower, upper])
            first.append(lower)
        self.bufs = {}
        for r in keep:
            other = after(got[r], *hold) if hold else got[r]
            total = keep[r].astype(f32) + other.astype(f32)
            self.bufs[r] = total.astype(b16) if rest else total
        self.done += 1
        return first

    def finish(self):
        while self.done < len(self.order):
            self.step()
        return self.bufs[0][0]


def shift_outer(values, by):
    size = lax.axis_size("ctx")
    return lax.ppermute(
        values, "ctx", [(i, i + 2 * by) for i in range(size) if 0 <= i + 2 * by < size]
    )


def dot(a, b, dims):
    return lax.dot_general(a, b, (dims, ((), ())), preferred_element_type=f32)


def fill_bias(blocks, tokens, place, seg_refs, bias):
    queries = jnp.broadcast_to(seg_refs[0][0:1, :].astype(f32), (tokens, tokens))
    for j in range(blocks):
        keys = jnp.broadcast_to(seg_refs[j][0:1, :].astype(f32), (tokens, tokens)).T
        allowed = (keys == queries) & (place >= j)
        if j == 0:
            key_row = lax.broadcasted_iota(jnp.int32, (tokens, tokens), 0)
            query_col = lax.broadcasted_iota(jnp.int32, (tokens, tokens), 1)
            allowed = allowed & (key_row <= query_col)
        bias[j * tokens : (j + 1) * tokens, :] = jnp.where(allowed, 0.0, masked)


def heads_side(ref):
    return jnp.concatenate(
        [ref[h * HEAD_DIM : (h + 1) * HEAD_DIM, :] for h in range(GROUP)], axis=1
    )


def forward_kernel(blocks, tokens, place_ref, *refs):
    q_ref = refs[0]
    k_refs = refs[1 : 1 + blocks]
    v_refs = refs[1 + blocks : 1 + 2 * blocks]
    seg_refs = refs[1 + 2 * blocks : 1 + 3 * blocks]
    att_ref, lse_ref, bias = refs[1 + 3 * blocks :]

    @pl.when(pl.program_id(1) == 0)
    def _():
        fill_bias(blocks, tokens, place_ref[0], seg_refs, bias)

    keys = jnp.concatenate([r[...] for r in k_refs], axis=1)
    values = jnp.concatenate([r[...] for r in v_refs], axis=1)
    scores = dot(keys, heads_side(q_ref), ((0,), (0,)))
    for h in range(GROUP):
        own = scores[:, h * tokens : (h + 1) * tokens] + bias[...]
        top = jnp.max(own, axis=0, keepdims=True)
        probs = jnp.exp(own - top)
        total = jnp.sum(probs, axis=0, keepdims=True)
        out = dot(values, probs.astype(b16), ((1,), (0,)))
        att_ref[h * HEAD_DIM : (h + 1) * HEAD_DIM, :] = (out / total).astype(b16)
        lse_ref[0, h : h + 1, :] = top + jnp.log(total)


def backward_kernel(blocks, tokens, place_ref, *refs):
    q_ref, datt_ref, lse_ref = refs[:3]
    k_refs = refs[3 : 3 + blocks]
    v_refs = refs[3 + blocks : 3 + 2 * blocks]
    seg_refs = refs[3 + 2 * blocks : 3 + 3 * blocks]
    dq_ref = refs[3 + 3 * blocks]
    dkv_refs = refs[4 + 3 * blocks : 4 + 4 * blocks]
    bias, p_scr, ds_scr = refs[4 + 4 * blocks :]

    @pl.when(pl.program_id(1) == 0)
    def _():
        fill_bias(blocks, tokens, place_ref[0], seg_refs, bias)

    keys = jnp.concatenate([r[...] for r in k_refs], axis=1)
    values = jnp.concatenate([r[...] for r in v_refs], axis=1)
    queries = heads_side(q_ref)
    grads = heads_side(datt_ref)
    scores = dot(keys, queries, ((0,), (0,)))
    d_probs = dot(values, grads, ((0,), (0,)))
    for h in range(GROUP):
        lanes = slice(h * tokens, (h + 1) * tokens)
        probs = jnp.exp(scores[:, lanes] + bias[...] - lse_ref[0, h : h + 1, :])
        weighted = probs * d_probs[:, lanes]
        delta = jnp.sum(weighted, axis=0, keepdims=True)
        p_scr[:, lanes] = probs.astype(b16)
        ds_scr[:, lanes] = (weighted - probs * delta).astype(b16)
    d_scores = ds_scr[...]
    dq = dot(keys, d_scores, ((1,), (0,)))
    for h in range(GROUP):
        dq_ref[h * HEAD_DIM : (h + 1) * HEAD_DIM, :] = dq[:, h * tokens : (h + 1) * tokens]
    dk = dot(queries, d_scores, ((1,), (1,)))
    dv = dot(grads, p_scr[...], ((1,), (1,)))
    for j in range(blocks):
        lanes = slice(j * tokens, (j + 1) * tokens)
        dkv_refs[j][0] = dk[:, lanes].astype(b16)
        dkv_refs[j][1] = dv[:, lanes].astype(b16)


def kv_specs(blocks, tokens):
    per_group = (HEAD_DIM, tokens)
    key = pl.BlockSpec(per_group, lambda s, g, _: (g, s))
    value = pl.BlockSpec(per_group, lambda s, g, _: (KEY_VALUE_HEADS + g, s))
    seg_row = 2 * KEY_VALUE_HEADS * HEAD_DIM // 16
    seg = pl.BlockSpec((16, tokens), lambda s, g, _: (seg_row, s))
    return [key] * blocks + [value] * blocks + [seg] * blocks


def attend(place, q_rot, pieces, sequences, tokens):
    blocks = len(pieces)
    heads = pl.BlockSpec((GROUP * HEAD_DIM, tokens), lambda s, g, _: (g, s))
    stat = pl.BlockSpec((1, 8, tokens), lambda s, g, _: (g, 0, s))
    wide = sequences * tokens
    return pl.pallas_call(
        functools.partial(forward_kernel, blocks, tokens),
        grid_spec=pltpu.PrefetchScalarGridSpec(
            num_scalar_prefetch=1,
            grid=(sequences, KEY_VALUE_HEADS),
            in_specs=[heads] + kv_specs(blocks, tokens),
            out_specs=[heads, stat],
            scratch_shapes=[pltpu.VMEM((blocks * tokens, tokens), f32)],
        ),
        out_shape=[
            jax.ShapeDtypeStruct((QUERY_HEADS * HEAD_DIM, wide), b16),
            jax.ShapeDtypeStruct((KEY_VALUE_HEADS, 8, wide), f32),
        ],
        compiler_params=pltpu.CompilerParams(vmem_limit_bytes=40 << 20),
        cost_estimate=pl.CostEstimate(flops=1, bytes_accessed=1, transcendentals=0),
        name="attend",
    )(place, q_rot, *pieces, *pieces, *pieces)


def attend_back(place, q_rot, datt, lse, pieces, sequences, tokens):
    blocks = len(pieces)
    heads = pl.BlockSpec((GROUP * HEAD_DIM, tokens), lambda s, g, _: (g, s))
    stat = pl.BlockSpec((1, 8, tokens), lambda s, g, _: (g, 0, s))
    pair = pl.BlockSpec((2, HEAD_DIM, tokens), lambda s, g, _: (0, g, s))
    wide = sequences * tokens
    return pl.pallas_call(
        functools.partial(backward_kernel, blocks, tokens),
        grid_spec=pltpu.PrefetchScalarGridSpec(
            num_scalar_prefetch=1,
            grid=(sequences, KEY_VALUE_HEADS),
            in_specs=[heads, heads, stat] + kv_specs(blocks, tokens),
            out_specs=[heads] + [pair] * blocks,
            scratch_shapes=[
                pltpu.VMEM((blocks * tokens, tokens), f32),
                pltpu.VMEM((blocks * tokens, GROUP * tokens), b16),
                pltpu.VMEM((blocks * tokens, GROUP * tokens), b16),
            ],
        ),
        out_shape=[jax.ShapeDtypeStruct((QUERY_HEADS * HEAD_DIM, wide), f32)]
        + [jax.ShapeDtypeStruct((2, KEY_VALUE_HEADS * HEAD_DIM, wide), b16)] * blocks,
        compiler_params=pltpu.CompilerParams(vmem_limit_bytes=48 << 20),
        cost_estimate=pl.CostEstimate(flops=1, bytes_accessed=1, transcendentals=0),
        name="attend_back",
    )(place, q_rot, datt, lse, *pieces, *pieces, *pieces)


def turned(low, high, cosine, sine, sign):
    return low * cosine - sign * high * sine, high * cosine + sign * low * sine


def turn_rows(source, target, heads, cosine, sine, sign, scale):
    for h in range(heads):
        at = h * HEAD_DIM
        low, high = source[at : at + HALF], source[at + HALF : at + HEAD_DIM]
        pair = turned(low, high, cosine, sine, sign)
        for i, half in enumerate(pair):
            rows = slice(at + i * HALF, at + (i + 1) * HALF)
            target[rows] = (half * scale).astype(target.dtype)


def project_kv_kernel(parts, kv_cols, ctx, *refs):
    x_ref, inv_ref, gain_ref = refs[:3]
    w_refs = refs[3 : 3 + parts]
    seg_ref, cos_ref, sin_ref, normed_ref, own_ref, blocks, flat = refs[3 + parts :]
    for r in range(parts):
        normed = (x_ref[r].astype(f32) * inv_ref[...] * gain_ref[r]).astype(b16)
        normed_ref[r] = normed
        part = dot(w_refs[r][...], normed, ((1,), (0,)))
        if r == 0:
            blocks[...] = part
        else:
            blocks[...] += part
    rows = blocks.shape[0] // ctx
    kv_width = KEY_VALUE_HEADS * HEAD_DIM
    for c in range(ctx):
        base, at = c * rows, c * kv_cols
        flat[at : at + kv_cols] = blocks[base : base + kv_cols]
        at += kv_width
        flat[at : at + kv_cols] = blocks[base + kv_cols : base + 2 * kv_cols]
    turn_rows(flat, own_ref, KEY_VALUE_HEADS, cos_ref[...], sin_ref[...], 1.0, 1.0)
    own_ref[kv_width : 2 * kv_width] = flat[kv_width : 2 * kv_width].astype(b16)
    own_ref[2 * kv_width : 2 * kv_width + 16] = seg_ref[...]


def project_q_kernel(parts, scale, normed_ref, cos_ref, sin_ref, *refs):
    w_refs = refs[:parts]
    q_ref, flat = refs[parts:]
    acc = dot(w_refs[0][...], normed_ref[0], ((1,), (0,)))
    for r in range(1, parts):
        acc = acc + dot(w_refs[r][...], normed_ref[r], ((1,), (0,)))
    flat[...] = acc
    turn_rows(flat, q_ref, QUERY_HEADS, cos_ref[...], sin_ref[...], 1.0, scale)


def project_q_back_kernel(parts, scale, dq_ref, normed_ref, cos_ref, sin_ref, *refs):
    w_refs = refs[:parts]
    dn_ref = refs[parts]
    g_refs = refs[1 + parts : 1 + 2 * parts]
    flat = refs[1 + 2 * parts]
    turn_rows(dq_ref, flat, QUERY_HEADS, cos_ref[...], sin_ref[...], -1.0, scale)
    for r in range(parts):
        g_refs[r][...] = dot(flat[...], normed_ref[r], ((1,), (1,))).astype(b16)
    for r in range(parts):
        dn_ref[r] = dot(w_refs[r][...], flat[...], ((0,), (0,)))


def project_kv_back_kernel(parts, kv_cols, ctx, me_ref, *refs):
    dkv_ref, cos_ref, sin_ref, normed_ref, dn_q_ref, x_ref, inv_ref, gain_ref, d_mid_ref = refs[:9]
    w_refs = refs[9 : 9 + parts]
    out_ref, g_gain_ref = refs[9 + parts : 11 + parts]
    g_refs = refs[11 + parts : 11 + 2 * parts]
    flat, blocks, d_x = refs[11 + 2 * parts :]
    kv_width = KEY_VALUE_HEADS * HEAD_DIM
    turn_rows(dkv_ref.at[0], flat, KEY_VALUE_HEADS, cos_ref[...], sin_ref[...], -1.0, 1.0)
    rows = blocks.shape[0] // ctx
    for c in range(ctx):
        base, at = c * rows, c * kv_cols
        blocks[base : base + kv_cols] = flat[at : at + kv_cols]
        blocks[base + kv_cols : base + 2 * kv_cols] = dkv_ref[1, at : at + kv_cols]
        blocks[base + 2 * kv_cols : base + rows] = jnp.zeros(
            (rows - 2 * kv_cols, blocks.shape[1]), f32
        )
    low = blocks[...].astype(b16)
    for r in range(parts):
        g_refs[r][...] = dot(low, normed_ref[r], ((1,), (1,))).astype(b16)
    inv = inv_ref[...]
    mean = jnp.zeros_like(inv)
    for r in range(parts):
        d_normed = dn_q_ref[r] + dot(w_refs[r][...], low, ((0,), (0,)))
        x = x_ref[r].astype(f32)
        g_gain_ref[r] = jnp.sum(d_normed * (x * inv), axis=1, keepdims=True)
        scaled = d_normed * gain_ref[r]
        d_x[r] = scaled
        mean = mean + jnp.sum(scaled * x, axis=0, keepdims=True)
    mean = mean / (parts * x_ref.shape[1]) * (inv * inv * inv)
    features, tokens = x_ref.shape[1], out_ref.shape[2]
    for d in range(parts):
        r = me_ref[0] ^ d
        total = d_mid_ref[d] + inv * d_x[r] - x_ref[r].astype(f32) * mean
        for s in range(out_ref.shape[0]):
            lanes = slice(s * tokens, (s + 1) * tokens)
            out_ref[s, d * features : (d + 1) * features] = total[:, lanes].astype(b16)


def mix_kernel(parts, me_ref, att_ref, x_ref, gain_ref, *refs):
    w_refs = refs[:parts]
    mid_ref, inv_ref, normed_ref, normed_t_ref = refs[parts:]
    mid = x_ref[...].astype(f32)
    for r in range(parts):
        mid = mid + dot(att_ref[me_ref[0] ^ r], w_refs[r][...], ((0,), (1,)))
    mid_ref[...] = mid
    inv = lax.rsqrt(jnp.mean(mid * mid, axis=-1, keepdims=True) + epsilon)
    inv_ref[...] = inv
    normed = mid * inv * gain_ref[...]
    rows = normed_ref.shape[2]
    for d in range(parts):
        part = normed[:, d * rows : (d + 1) * rows]
        normed_ref[me_ref[0] ^ d] = part.astype(b16)
        normed_t_ref[me_ref[0] ^ d] = part.T.astype(b16)


def mix_back_kernel(parts, me_ref, att_ref, cot_ref, mid_ref, inv_ref, gain_ref, dn_ref, *refs):
    w_refs = refs[:parts]
    datt_ref, d_mid_ref, g_gain_ref = refs[parts : 3 + parts]
    g_refs = refs[3 + parts : 3 + 2 * parts]
    flipped = refs[3 + 2 * parts]
    rows = dn_ref.shape[2]
    inv = inv_ref[...]
    mean = jnp.zeros_like(inv)
    for d in range(parts):
        lanes = slice(d * rows, (d + 1) * rows)
        d_normed = dn_ref[me_ref[0] ^ d]
        mid = mid_ref[:, lanes]
        g_gain_ref[d] = jnp.sum(d_normed * (mid * inv), axis=0, keepdims=True)
        mean = mean + jnp.sum(d_normed * gain_ref[:, lanes] * mid, axis=-1, keepdims=True)
    mean = mean / (parts * rows) * (inv * inv * inv)
    for d in range(parts):
        lanes = slice(d * rows, (d + 1) * rows)
        scaled = dn_ref[me_ref[0] ^ d] * gain_ref[:, lanes]
        d_mid = (inv * scaled - mid_ref[:, lanes] * mean).T
        cot = [cot_ref[s, lanes].astype(f32) for s in range(cot_ref.shape[0])]
        d_mid = d_mid + jnp.concatenate(cot, axis=1)
        d_mid_ref[d] = d_mid
        flipped[lanes] = d_mid.astype(b16)
    for r in range(parts):
        at = me_ref[0] ^ r
        g_refs[r][...] = dot(flipped[...], att_ref[at], ((1,), (1,))).astype(b16)
        datt_ref[at] = dot(w_refs[r][...], flipped[...], ((0,), (0,))).astype(b16)


def ffn_kernel(parts, per, me_ref, n_ref, nt_ref, cot_ref, mid_ref, *refs):
    f_refs = [refs[:parts], refs[parts : 2 * parts]]
    d_refs = refs[2 * parts : 3 * parts]
    out_ref, dn_ref = refs[3 * parts : 3 * parts + 2]
    rest = refs[3 * parts + 2 :]
    gf_refs = [rest[:parts], rest[parts : 2 * parts]]
    gd_refs = rest[2 * parts : 3 * parts]
    acc, down, g_down, hidden, cot_t, cot = rest[3 * parts :]
    step = pl.program_id(0)
    for r in range(parts):

        @pl.when(step == r)
        def _(r=r):
            down[...] = d_refs[r][...]

    @pl.when(step == 0)
    def _():
        acc[...] = jnp.zeros_like(acc)
        length = cot_ref.shape[2]
        for s in range(cot_ref.shape[0]):
            cot_t[:, s * length : (s + 1) * length] = cot_ref[s]
            cot[s * length : (s + 1) * length, :] = cot_ref[s].T
        dn_ref[...] = jnp.zeros_like(dn_ref)

    cut = f_refs[0][0].shape[2]
    ff = (cut + f_refs[1][0].shape[2]) // 2
    d_hidden = dot(cot[...], down[...], ((1,), (0,)))
    for i in range(per):
        both = []
        for side in f_refs:
            part = dot(n_ref[0], side[0][i], ((1,), (0,)))
            for r in range(1, parts):
                part = part + dot(n_ref[r], side[r][i], ((1,), (0,)))
            both.append(part)
        both = jnp.concatenate(both, axis=1)
        gate, up = both[:, :ff], both[:, ff:]
        grad = d_hidden[:, i * ff : (i + 1) * ff]
        sigma = jax.nn.sigmoid(gate)
        silu = gate * sigma
        hidden[:, i * ff : (i + 1) * ff] = (silu * up).astype(b16)
        d_gate = grad * up * (sigma * (1.0 + gate * (1.0 - sigma)))
        d_both = jnp.concatenate([d_gate, grad * silu], axis=1).astype(b16)
        sides = (d_both[:, :cut], d_both[:, cut:])
        for r in range(parts):
            for side in range(2):
                grad = dot(nt_ref[r], sides[side], ((1,), (0,)))
                gf_refs[side][r][i] = grad.astype(b16)
            dn_ref[r] += dot(sides[0], f_refs[0][r][i], ((1,), (1,))) + dot(
                sides[1], f_refs[1][r][i], ((1,), (1,))
            )
    acc[...] += dot(hidden[...], down[...], ((1,), (1,)))
    g_down[...] = dot(cot_t[...], hidden[...], ((1,), (0,))).astype(b16)
    for r in range(parts):

        @pl.when(step == r)
        def _(r=r):
            gd_refs[r][...] = g_down[...]

    @pl.when(step == parts - 1)
    def _():
        length = out_ref.shape[2]
        for s in range(out_ref.shape[0]):
            part = slice(s * length, (s + 1) * length)
            out_ref[s] = (mid_ref[part] + acc[part]).T.astype(b16)


def ffn(me, n_rel, nt_rel, cot, mid, f_one, f_two, d_list):
    parts = len(f_one)
    ctx, rows, cut = f_one[0].shape
    wide = cut + f_two[0].shape[2]
    per = ctx // parts
    tokens, width = mid.shape
    down_shape = d_list[0].shape

    def whole(a):
        return pl.BlockSpec(a.shape, lambda i, me: (0,) * a.ndim, pipeline_mode=pl.Buffered(1))

    f_specs = [
        pl.BlockSpec((per, rows, n), lambda i, me: (me[0] ^ i, 0, 0))
        for n in [cut] * parts + [wide - cut] * parts
    ]
    out_shape = [
        jax.ShapeDtypeStruct(cot.shape, b16),
        jax.ShapeDtypeStruct((parts, tokens, rows), f32),
    ]
    out_shape += [jax.ShapeDtypeStruct(f.shape, b16) for f in f_one + f_two]
    out_shape += [jax.ShapeDtypeStruct(down_shape, b16)] * parts
    return pl.pallas_call(
        functools.partial(ffn_kernel, parts, per),
        grid_spec=pltpu.PrefetchScalarGridSpec(
            num_scalar_prefetch=1,
            grid=(parts,),
            in_specs=[whole(a) for a in (n_rel, nt_rel, cot, mid)]
            + f_specs
            + [whole(a) for a in d_list],
            out_specs=[whole(a) for a in out_shape[:2]]
            + f_specs
            + [whole(a) for a in d_list],
            scratch_shapes=[
                pltpu.VMEM((tokens, width), f32),
                pltpu.VMEM(down_shape, b16),
                pltpu.VMEM(down_shape, b16),
                pltpu.VMEM((tokens, per * wide // 2), b16),
                pltpu.VMEM((width, tokens), b16),
                pltpu.VMEM((tokens, width), b16),
            ],
        ),
        out_shape=out_shape,
        compiler_params=pltpu.CompilerParams(vmem_limit_bytes=58 << 20),
        cost_estimate=pl.CostEstimate(flops=1, bytes_accessed=1, transcendentals=0),
        name="ffn",
    )(me, n_rel, nt_rel, cot, mid, *f_one, *f_two, *d_list)


def in_vmem(kernel, name, out_shape, scratch, *args, scalars=0):
    vmem = pl.BlockSpec(memory_space=pltpu.VMEM)
    smem = pl.BlockSpec(memory_space=pltpu.SMEM)
    return pl.pallas_call(
        kernel,
        in_specs=[smem] * scalars + [vmem] * (len(args) - scalars),
        out_specs=[vmem] * len(out_shape),
        out_shape=out_shape,
        scratch_shapes=scratch,
        compiler_params=pltpu.CompilerParams(vmem_limit_bytes=48 << 20),
        cost_estimate=pl.CostEstimate(flops=1, bytes_accessed=1, transcendentals=0),
        name=name,
    )(*args)


def per_device(
    inputs,
    gain_one,
    query_weight,
    key_weight,
    value_weight,
    output_weight,
    gain_two,
    gate_weight,
    up_weight,
    down_weight,
    segment_ids,
    cotangent,
):
    dp, ctx = lax.axis_size("dp"), lax.axis_size("ctx")
    sequences, tokens, width = inputs.shape
    total = sequences * tokens
    rows = query_weight.shape[0]
    q_cols, kv_cols = query_weight.shape[1], key_weight.shape[1]
    ff_cols = gate_weight.shape[1]
    down_rows, out_cols = down_weight.shape
    kv_width = KEY_VALUE_HEADS * HEAD_DIM
    shape_of = jax.ShapeDtypeStruct

    dp_bits, ctx_bits = bits_of("dp", dp), bits_of("ctx", ctx)
    x_last = ctx_bits + dp_bits
    y_last = ctx_bits[:-1] + dp_bits[:-1] + ctx_bits[-1:] + dp_bits[-1:]
    z_last = ctx_bits[:-2] + ctx_bits[-1:] + dp_bits[:-1] + ctx_bits[-2:-1] + dp_bits[-1:]

    place = lax.axis_index("ctx")
    me = lax.axis_index("dp")
    me_arg = me.reshape(1).astype(jnp.int32)
    place_arg = place.reshape(1).astype(jnp.int32)

    def relative(stacked):
        return jnp.stack(
            [lax.dynamic_index_in_dim(stacked, me ^ r, 0, keepdims=False) for r in range(dp)]
        )

    gains = jnp.concatenate([gain_one, gain_two])
    gain_rows = -(-gains.size // rows)
    gains = jnp.pad(gains, (0, gain_rows * rows - gains.size)).reshape(gain_rows, rows)
    pad_rows = -(2 * kv_cols + gain_rows) % 8
    kv_block = jnp.concatenate(
        [key_weight.T, value_weight.T, gains, jnp.zeros((pad_rows, rows), b16)]
    )
    kv_gather = Gather(kv_block, y_last)
    qo_gather = Gather(jnp.concatenate([query_weight.T, output_weight.T]), x_last)
    gate_up = jnp.concatenate([gate_weight, up_weight], axis=1)
    cut = max(2 * ff_cols * 3 // 5 // 128, 1) * 128
    one_gather = Gather(gate_up[:, :cut], x_last)
    two_gather = Gather(gate_up[:, cut:], y_last)
    down_gather = Gather(down_weight.T, z_last)
    outer = len(ctx_bits) - 1
    token = kv_gather.step()
    one_gather.step(*token)
    two_gather.step(*token)
    token = kv_gather.step()
    down_gather.step(*token)
    qo_gather.step(*token)
    while kv_gather.done < len(x_last) - 1:
        token = kv_gather.step()
    for _ in range(outer - 1):
        two_gather.step(*token)
        down_gather.step(*token)
        one_gather.step(*token)
        qo_gather.step(*token)
    kv_gather.step()
    kv_all = kv_gather.result()

    first_gain = 2 * kv_cols
    gain_all = kv_all[0][:, first_gain : first_gain + gain_rows].reshape(ctx, -1)
    gain_part = gain_one.shape[0]
    gain_a = relative(gain_all[:, :gain_part].reshape(dp, rows, 1).astype(f32))
    gain_b = gain_all[:, gain_part : 2 * gain_part].reshape(1, width).astype(f32)
    kv_all = [a.reshape(-1, rows) for a in kv_all]

    cot = jnp.transpose(cotangent, (0, 2, 1))
    x_low = inputs.reshape(total, width)
    x = x_low.astype(f32)
    inv_one = lax.rsqrt(jnp.mean(x * x, axis=-1) + epsilon).reshape(1, total)
    x_t = relative(x_low.T.reshape(dp, rows, total))
    positions = (place * tokens + jnp.arange(tokens, dtype=jnp.int32)).astype(f32)
    positions = jnp.tile(positions, sequences)
    frequency = jnp.exp(jnp.arange(HALF, dtype=f32) * (-2.0 * math.log(rope_base) / HEAD_DIM))
    angles = frequency[:, None] * positions[None, :]
    cosine, sine = jnp.cos(angles), jnp.sin(angles)
    score_scale = HEAD_DIM ** (-0.5)
    seg_row = jnp.pad(segment_ids.reshape(1, total).astype(b16), ((0, 15), (0, 0)))
    block_rows = kv_all[0].shape[0]
    one_t, own = in_vmem(
        functools.partial(project_kv_kernel, dp, kv_cols, ctx),
        "project_kv",
        [shape_of((dp, rows, total), b16), shape_of((2 * kv_width + 16, total), b16)],
        [pltpu.VMEM((block_rows, total), f32), pltpu.VMEM((2 * kv_width, total), f32)],
        x_t,
        inv_one,
        gain_a,
        *kv_all,
        seg_row,
        cosine,
        sine,
    )

    steps = ctx // 4
    inner = bit("ctx", 1)
    straight = [own]
    for _ in range(steps):
        straight.append(shift_outer(straight[-1], 1))
    crossed = [
        swap(jnp.where(inner == 0, straight[k], straight[k + 1]), "ctx", 1) for k in range(steps)
    ]
    while two_gather.done < len(x_last) - 2:
        spread = two_gather.step()
    while down_gather.done < len(x_last) - 2:
        spread += down_gather.step()
    while one_gather.done < outer + 1:
        one_gather.step()
    while qo_gather.done < outer + 1:
        qo_gather.step()
    ahead = qo_gather.step(*spread)
    while qo_gather.done < len(x_last):
        qo_gather.step()
    q_all = [a[:, :q_cols].reshape(-1, rows) for a in qo_gather.result()]
    out_all = [a[:, q_cols:].reshape(-1, rows) for a in qo_gather.result()]
    (q_rot,) = in_vmem(
        functools.partial(project_q_kernel, dp, score_scale),
        "project_q",
        [shape_of((width, total), b16)],
        [pltpu.VMEM((width, total), f32)],
        after(one_t, straight[1]),
        cosine,
        sine,
        *q_all,
    )
    one_gather.step(*ahead, straight[1])
    down_gather.step(straight[steps])
    two_gather.step(*crossed)
    pieces = []
    for k in range(steps):
        pieces += [straight[k], crossed[k]]
    pieces.append(straight[steps])

    att, lse = attend(place_arg, q_rot, pieces, sequences, tokens)
    for g in (one_gather, two_gather, down_gather):
        while g.done < len(x_last):
            g.step(lse)
    down_all = [a.reshape(-1, down_rows) for a in down_gather.result()]
    att_3 = att.reshape(dp, rows, total)

    mid, inv_two, two, two_t = in_vmem(
        functools.partial(mix_kernel, dp),
        "mix",
        [
            shape_of((total, width), f32),
            shape_of((total, 1), f32),
            shape_of((dp, total, rows), b16),
            shape_of((dp, rows, total), b16),
        ],
        [],
        me_arg,
        att_3,
        x_low,
        gain_b,
        *out_all,
        scalars=1,
    )
    output, d_two, *grads = ffn(me_arg, two, two_t, cot, mid, one_gather.result(), two_gather.result(), down_all)
    g_one = Scatter(grads[:dp], x_last[::-1])
    g_two = Scatter(grads[dp : 2 * dp], y_last[::-1])
    g_down = Scatter([g.reshape(ctx, out_cols, down_rows) for g in grads[2 * dp :]], z_last[::-1])
    d_att, d_mid, g_gain_two, *g_out = in_vmem(
        functools.partial(mix_back_kernel, dp),
        "mix_back",
        [
            shape_of(att_3.shape, b16),
            shape_of((dp, rows, total), f32),
            shape_of((dp, 1, rows), f32),
        ]
        + [shape_of((width, rows), b16)] * dp,
        [pltpu.VMEM((width, total), b16)],
        me_arg,
        att_3,
        cot,
        mid,
        inv_two,
        gain_b,
        d_two,
        *out_all,
        scalars=1,
    )
    folded = g_one.step(hold=(d_att,))
    folded += [t for g in (g_two, g_down) for t in g.step(hold=(d_att, *folded[:1]))]
    d_att = after(d_att.reshape(width, total), *folded)
    under_x, under_y, under_z = g_one.step(), g_two.step(), g_down.step()
    dq_rot, *parts = attend_back(place_arg, q_rot, d_att, lse, pieces, sequences, tokens)
    dq_rot = after(dq_rot, *under_x, *under_y, *under_z)
    parts = [after(p, *under_y) for p in parts]
    dn_q, *g_q = in_vmem(
        functools.partial(project_q_back_kernel, dp, score_scale),
        "project_q_back",
        [shape_of((dp, rows, total), f32)] + [shape_of((width, rows), b16)] * dp,
        [pltpu.VMEM((width, total), b16)],
        dq_rot,
        one_t,
        cosine,
        sine,
        *q_all,
    )

    returned = [swap(parts[2 * k + 1], "ctx", 1).astype(f32) for k in range(steps)]
    here = []
    for k in range(steps + 1):
        value = parts[2 * k].astype(f32)
        if k < steps:
            value = value + jnp.where(inner == 0, returned[k], 0.0)
        if k > 0:
            value = value + jnp.where(inner == 1, returned[k - 1], 0.0)
        here.append(value)
    carried = after(here[steps], *under_x, *under_z)
    for k in range(steps, 0, -1):
        moved = shift_outer(carried.astype(b16), -1)
        if k == steps:
            first_moved = moved
        carried = here[k - 1] + moved.astype(f32)
    g_qo = [
        jnp.concatenate([q.reshape(ctx, q_cols, rows), o.reshape(ctx, out_cols, rows)], axis=1)
        for q, o in zip(g_q, g_out, strict=True)
    ]
    g_qo = Scatter(g_qo, x_last[::-1])
    g_qo.step(parts[0])
    beside = g_two.step(hold=(first_moved,)) + g_down.step(hold=(first_moved,))
    beside += g_one.step(*returned)
    ahead = g_qo.step(*beside[:2])
    for g in (g_two, g_down):
        g.step(first_moved)
    carried = after(carried, *beside)
    input_grad, g_gain_one, *g_kv = in_vmem(
        functools.partial(project_kv_back_kernel, dp, kv_cols, ctx),
        "project_kv_back",
        [shape_of((sequences, width, tokens), b16), shape_of((dp, rows, 1), f32)]
        + [shape_of((block_rows, rows), b16)] * dp,
        [
            pltpu.VMEM((kv_width, total), f32),
            pltpu.VMEM((block_rows, total), f32),
            pltpu.VMEM((dp, rows, total), f32),
        ],
        me_arg,
        carried,
        cosine,
        sine,
        one_t,
        dn_q,
        x_t,
        inv_one,
        gain_a,
        d_mid,
        *kv_all,
        scalars=1,
    )
    g_gains = jnp.concatenate(
        [relative(g_gain_one).reshape(ctx, gain_part), g_gain_two.reshape(ctx, gain_part)], axis=1
    ).astype(b16)
    g_gains = jnp.pad(g_gains, ((0, 0), (0, gain_rows * rows - 2 * gain_part)))
    g_gains = jnp.pad(g_gains.reshape(ctx, gain_rows, rows), ((0, 0), (0, pad_rows), (0, 0)))
    g_kv = [
        jnp.concatenate([g.reshape(ctx, -1, rows)[:, :first_gain], g_gains], axis=1) for g in g_kv
    ]
    g_kv = Scatter(g_kv, x_last[::-1])
    g_one.step(first_moved, hold=(input_grad,))
    token = g_kv.step(hold=ahead)
    g_qo.step()
    for g in (g_two, g_down, g_one):
        while g.done < len(x_last):
            g.step(hold=(input_grad,))
    while g_kv.done < len(x_last):
        token = g_kv.step(*token)
        if g_qo.done < min(g_kv.done, len(x_last)):
            g_qo.step(*token)
    g_kv, g_qo, g_down = g_kv.finish(), g_qo.finish(), g_down.finish()
    g_gu = jnp.concatenate([g_one.finish(), g_two.finish()], axis=1)
    g_gains = g_kv[first_gain : first_gain + gain_rows].reshape(-1)
    return (
        jnp.transpose(output, (0, 2, 1)),
        jnp.transpose(input_grad, (0, 2, 1)),
        g_gains[:gain_part],
        g_qo[:q_cols].T,
        g_kv[:kv_cols].T,
        g_kv[kv_cols : 2 * kv_cols].T,
        g_qo[q_cols:].T,
        g_gains[gain_part : 2 * gain_part],
        g_gu[:, :ff_cols],
        g_gu[:, ff_cols:],
        g_down.T,
    )


def solution(mesh):
    act = P("dp", "ctx", None)
    weight = P("dp", "ctx")
    gain = P("ctx")
    return jax.shard_map(
        per_device,
        mesh=mesh,
        in_specs=(
            act, gain, weight, weight, weight, weight, gain, weight, weight, weight, P("dp", "ctx"), act,
        ),
        out_specs=(
            act, act, gain, weight, weight, weight, weight, gain, weight, weight, weight,
        ),
        check_vma=False,
    )
```
